256 devices in a mesh: row: 8 (over x, core), col: 32 (over y, z).
Axes of the slice: x: 4, y: 4, z: 8, core: 2. Of those that a mesh axis runs over, the one named last changes fastest.
Arguments:
- amplitudes: float32 [262144, 1024], P(('row', 'col')), may hold values from -6 to 6
- integrals: float32 [262144, 1024], P(('row', 'col')), may hold values from -0.046875 to 0.046875
- denominators: float32 [1024, 1024], P('col', 'row'), may hold values from 1 to 4
- history: float32 [8, 1024, 1024], P(None, 'col', 'row'), may hold values from -80 to 80
Outputs:
- extrapolated: float32 [1024, 1024], P('col', 'row')
- coefficients: float32 [8], replicated
The draws below stay inside these ranges and needn't reach their ends.
All inputs are finite; a program needn't handle non-finite values.
Results may differ from the reference program's by a relative error of at most 0.00005.
Values sent between devices are 32-bit elements; how exact they have to be, the bound alone decides.
No kernel may reach another device: no remote copies, remote signals or barrier semaphores. Data moves between devices by JAX's collectives and lax.ppermute only.
A program may use at most 64 MiB of HBM per device.

```python
import jax
import jax.numpy as jnp
from jax import lax

OCC = 32
VBLK = 32
HIST = 8
CD = 262144
IJ = 1024
AB = 1024


def draw_history(key, part):
    keys = jax.random.split(jax.random.fold_in(key, 7), 1)
    base = jnp.clip(jax.random.normal(keys[0], (HIST, OCC * OCC, VBLK * VBLK), jnp.float32), -5.0, 5.0)
    pair_ij = jnp.arange(OCC * OCC, dtype=jnp.float32)[:, None] / (OCC * OCC)
    pair_ab = jnp.arange(VBLK * VBLK, dtype=jnp.float32)[None, :] / (VBLK * VBLK)
    ramp = 3.0 ** (0.5 * pair_ij + 0.5 * pair_ab)
    return base * ramp


def raised(entries, own_key, source, target, shards_of, factor):
    def block_of(axis_at):
        return (jnp.arange(entries.shape[axis_at]) // (entries.shape[axis_at] // shards_of)).reshape((-1,) + (1,) * (entries.ndim - 1 - axis_at))

    one_side = jax.random.permutation(own_key, shards_of)[block_of(target)]
    second = (block_of(target) + shards_of // 2) % shards_of
    return jnp.where((block_of(source) == one_side) | (block_of(source) == second), factor * entries, entries)


def shard_levels(rng, dims, pieces, least, high):
    loudness, own = 1.0, jax.random.fold_in(rng, 6)
    for axis_at, blocks in pieces:
        draws = jnp.exp(jax.random.uniform(jax.random.fold_in(own, axis_at), (blocks,), jnp.float32, least / len(pieces), high / len(pieces)))
        loudness = loudness * jnp.repeat(draws, dims[axis_at] // blocks).reshape([-1 if axis == axis_at else 1 for axis in range(len(dims))])
    return loudness


def noise(rng, extent, spread, limit, cuts=(), held_as=jnp.bfloat16):
    array = spread * jax.random.normal(rng, extent, jnp.float32)
    if cuts:
        array = array * shard_levels(rng, extent, cuts, -0.22, 0.18)
    return jnp.clip(array, -limit, limit).astype(held_as)


def bell_draw_with(rng, dims, width, bound, shards, heavy, kind=jnp.bfloat16):
    array = width * jax.random.normal(rng, dims, jnp.float32)
    if shards:
        array = array * shard_levels(rng, dims, shards, -0.22, 0.18)
    return jnp.clip(raised(array, jax.random.fold_in(rng, 3), *heavy), -bound, bound).astype(kind)


def setup_inputs(seed: int = 0) -> dict:
    arg_keys = jax.random.split(jax.random.key(seed), 5)
    amplitudes = noise(arg_keys[0], (CD, IJ), 1.0, 6.0, ((0, 256),), jnp.float32)
    integrals = bell_draw_with(arg_keys[1], (CD, AB), CD ** -0.5, 0.046875, ((0, 256),), (0, 1, 256, 6.0), jnp.float32)
    denominators = jnp.clip(1.0 + 3.0 * jax.random.uniform(arg_keys[2], (IJ, AB), jnp.float32) ** shard_levels(arg_keys[2], (IJ, AB), ((0, 32), (1, 8)), -0.2, 0.2), 1.0, 4.0)
    history = draw_history(jax.random.fold_in(arg_keys[4], 71), 0)
    return {"amplitudes": amplitudes, "integrals": integrals, "denominators": denominators, "history": history}


def flip(field):
    return field.reshape(OCC, OCC, VBLK, VBLK).transpose(1, 0, 3, 2).reshape(OCC * OCC, VBLK * VBLK)

def weights_of(gram):
    count = gram.shape[0]
    ridge = 1e-06 * jnp.trace(gram) / count
    factor = jnp.linalg.cholesky(gram + ridge * jnp.eye(count, dtype=gram.dtype))
    ones = jnp.ones((count, 1), gram.dtype)
    half = lax.linalg.triangular_solve(factor, ones, left_side=True, lower=True)
    whole = lax.linalg.triangular_solve(factor, half, left_side=True, lower=True, transpose_a=True)
    return whole[:, 0] / jnp.sum(whole)

def reference(amplitudes, integrals, denominators, history):
    ladder = lax.dot_general(amplitudes.astype(jnp.float32), integrals.astype(jnp.float32), (((0,), (0,)), ((), ())), precision=lax.Precision.HIGHEST, preferred_element_type=jnp.float32)
    symmetric = ladder + flip(ladder)
    update = symmetric / denominators
    following = jnp.concatenate([history[1:], update[None]], axis=0)
    errors = following - history
    gram = jnp.einsum('kxy,lxy->kl', errors, errors, precision=lax.Precision.HIGHEST)
    coefficients = weights_of(gram)
    extrapolated = jnp.einsum('k,kxy->xy', coefficients, following, precision=lax.Precision.HIGHEST)
    return (extrapolated, coefficients)
```

```python
import jax
import jax.numpy as jnp
from jax import lax
from jax.experimental import pallas as pl
from jax.experimental.pallas import tpu as pltpu
from jax.sharding import Mesh, PartitionSpec as P

OCC = 32
VBLK = 32
PAIRS = 1024
LANES = 128
ROWS = 256
STEPS = PAIRS // ROWS
HIST = 8


def mirror_kernel(other, p_ref, out_ref, onehot, halves, own, turned):
    step = pl.program_id(0)
    x = lax.axis_index("x")
    side = lax.axis_index("core")
    if other:
        side = 1 - side

    def group(d):
        return 2 * lax.rem(x + d, 4) + side

    @pl.when(step == 0)
    def _():
        source = lax.broadcasted_iota(jnp.int32, (PAIRS, LANES), 0)
        lane = lax.broadcasted_iota(jnp.int32, (PAIRS, LANES), 1)
        for d in range(4):
            target = group(d) * LANES + lane
            wanted = (target % VBLK) * VBLK + target // VBLK
            hot = jnp.where(source == wanted, 1.0, 0.0).astype(jnp.bfloat16)
            onehot[:PAIRS, d * LANES:(d + 1) * LANES] = hot
            onehot[PAIRS:, d * LANES:(d + 1) * LANES] = hot

    @pl.when(step < STEPS)
    def _():
        rows = pl.ds(pl.multiple_of(step * ROWS, ROWS), ROWS)
        p = p_ref[...]
        high = p.astype(jnp.bfloat16)
        halves[:, :PAIRS] = high
        halves[:, PAIRS:] = (p - high.astype(jnp.float32)).astype(jnp.bfloat16)
        flipped = jnp.dot(halves[...], onehot[...], preferred_element_type=jnp.float32)
        for d in range(4):
            turned[d, rows, :] = flipped[:, d * LANES:(d + 1) * LANES]
            own[d, rows, :] = p_ref[:, pl.ds(pl.multiple_of(group(d) * LANES, LANES), LANES)]

    @pl.when(step >= STEPS)
    def _():
        for k in range(ROWS // OCC):
            i = (step - STEPS) * (ROWS // OCC) + k
            mine = pl.ds(pl.multiple_of(i * OCC, OCC), OCC)
            for d in range(4):
                out_ref[d, k * OCC:(k + 1) * OCC, :] = own[d, mine, :] + turned[d, pl.ds(i, OCC, stride=OCC), :]


def mirrored(partial, other):
    def kernel(*refs):
        mirror_kernel(other, *refs)

    return pl.pallas_call(
        kernel,
        grid=(2 * STEPS,),
        in_specs=[pl.BlockSpec((ROWS, PAIRS), lambda m: (jnp.minimum(m, STEPS - 1), 0))],
        out_specs=pl.BlockSpec((4, ROWS, LANES), lambda m: (0, jnp.maximum(m - STEPS, 0), 0)),
        out_shape=jax.ShapeDtypeStruct((4, PAIRS, LANES), jnp.float32),
        scratch_shapes=[
            pltpu.VMEM((2 * PAIRS, 4 * LANES), jnp.bfloat16),
            pltpu.VMEM((ROWS, 2 * PAIRS), jnp.bfloat16),
            pltpu.VMEM((4, PAIRS, LANES), jnp.float32),
            pltpu.VMEM((4, PAIRS, LANES), jnp.float32),
        ],
        compiler_params=pltpu.CompilerParams(vmem_limit_bytes=24 * 2**20),
        cost_estimate=pl.CostEstimate(flops=2 * 2 * PAIRS * PAIRS * 512, bytes_accessed=6 * 2**20, transcendentals=0),
        name="mirror_other" if other else "mirror_own",
    )(partial)


def gram_kernel(parts_ref, den_ref, hist_ref, update_ref, message_ref):
    total = parts_ref[0]
    for s in range(1, 32):
        total = total + parts_ref[s]
    update = total / den_ref[...]
    update_ref[...] = update
    errors = [hist_ref[k + 1] - hist_ref[k] for k in range(HIST - 1)] + [update - hist_ref[HIST - 1]]
    lane = lax.broadcasted_iota(jnp.int32, (8, LANES), 1)
    message = jnp.zeros((8, LANES), jnp.float32)
    for k in range(HIST):
        for l in range(k + 1):
            value = jnp.sum(errors[k] * errors[l], keepdims=True)
            message = jnp.where(lane == HIST * k + l, value, message)
    for s in range(32):
        message_ref[s * 8:(s + 1) * 8, :] = message


def tail_kernel(grams_ref, update_ref, hist_ref, out_ref, coef_ref):
    row = jnp.sum(grams_ref[...], axis=0, keepdims=True)
    a = [[row[:, HIST * k + l:HIST * k + l + 1] for l in range(k + 1)] for k in range(HIST)]
    trace = a[0][0]
    for k in range(1, HIST):
        trace = trace + a[k][k]
    ridge = 1e-06 * trace / HIST
    for k in range(HIST):
        a[k][k] = a[k][k] + ridge
    low = [[None] * HIST for _ in range(HIST)]
    inverse = [None] * HIST
    for k in range(HIST):
        pivot = a[k][k]
        for m in range(k):
            pivot = pivot - low[k][m] * low[k][m]
        inverse[k] = 1.0 / jnp.sqrt(pivot)
        for n in range(k + 1, HIST):
            entry = a[n][k]
            for m in range(k):
                entry = entry - low[n][m] * low[k][m]
            low[n][k] = entry * inverse[k]
    half = [None] * HIST
    for k in range(HIST):
        value = jnp.ones((1, 1), jnp.float32)
        for m in range(k):
            value = value - low[k][m] * half[m]
        half[k] = value * inverse[k]
    whole = [None] * HIST
    for k in reversed(range(HIST)):
        value = half[k]
        for m in range(k + 1, HIST):
            value = value - low[m][k] * whole[m]
        whole[k] = value * inverse[k]
    total = whole[0]
    for k in range(1, HIST):
        total = total + whole[k]
    lane = lax.broadcasted_iota(jnp.int32, (1, HIST), 1)
    weights = [whole[k] / total for k in range(HIST)]
    coefficients = jnp.zeros((1, HIST), jnp.float32)
    for k in range(HIST):
        coefficients = jnp.where(lane == k, weights[k], coefficients)
    coef_ref[...] = coefficients
    out = weights[HIST - 1] * update_ref[...]
    for k in range(HIST - 1):
        out = out + weights[k] * hist_ref[k + 1]
    out_ref[...] = out


def shards(amplitudes, integrals, denominators, history):
    partial = lax.dot_general(
        amplitudes,
        integrals,
        (((0,), (0,)), ((), ())),
        precision=lax.Precision.HIGH,
        preferred_element_type=jnp.float32,
    )
    sent = mirrored(partial, True)
    came = lax.ppermute(sent, "core", [(0, 1), (1, 0)])
    kept = mirrored(partial, False)
    pieces = [kept[d] + came[d] for d in range(4)]
    arrived = [lax.ppermute(pieces[d], "x", [(i, (i + d) % 4) for i in range(4)]) for d in (2, 1, 3)]
    block = (pieces[0] + arrived[0]) + (arrived[1] + arrived[2])
    parts = lax.all_to_all(block, ("y", "z"), 0, 0, tiled=True).reshape(32, OCC, LANES)
    update, message = pl.pallas_call(
        gram_kernel,
        out_shape=(
            jax.ShapeDtypeStruct((OCC, LANES), jnp.float32),
            jax.ShapeDtypeStruct((256, LANES), jnp.float32),
        ),
        name="gram",
    )(parts, denominators, history)
    grams = lax.all_to_all(message, ("x", "core", "y", "z"), 0, 0, tiled=True)
    extrapolated, coefficients = pl.pallas_call(
        tail_kernel,
        out_shape=(
            jax.ShapeDtypeStruct((OCC, LANES), jnp.float32),
            jax.ShapeDtypeStruct((1, HIST), jnp.float32),
        ),
        name="tail",
    )(grams, update, history)
    return extrapolated, coefficients.reshape(HIST)


def solution(mesh):
    cores = Mesh(mesh.devices.reshape(4, 2, 4, 8), ("x", "core", "y", "z"))
    pairs = P(("x", "core", "y", "z"), None)
    return jax.shard_map(
        shards,
        mesh=cores,
        in_specs=(pairs, pairs, P(("y", "z"), ("x", "core")), P(None, ("y", "z"), ("x", "core"))),
        out_specs=(P(("y", "z"), ("x", "core")), P()),
        check_vma=False,
    )
```

```python
import jax
import jax.numpy as jnp
from jax import lax
from jax.experimental import pallas as pl
from jax.experimental.pallas import tpu as pltpu
from jax.sharding import Mesh, PartitionSpec as P

OCC = 32
VBLK = 32
PAIRS = 1024
LANES = 128
HALF = OCC // 2
HIST = 8
CHUNK = 256

SMALL = pltpu.CompilerParams(vmem_limit_bytes=4 * 2**20)


def mirror_kernel(part, p_ref, sent_ref, kept_ref, onehot, turned):
    x = lax.axis_index("x")
    y = lax.axis_index("y")
    core = lax.axis_index("core")
    source = lax.broadcasted_iota(jnp.int32, (PAIRS, LANES), 0)
    lane = lax.broadcasted_iota(jnp.int32, (PAIRS, LANES), 1)
    for g in range(8):
        target = g * LANES + lane
        wanted = (target % VBLK) * VBLK + target // VBLK
        onehot[:, g * LANES:(g + 1) * LANES] = jnp.where(source == wanted, 1.0, 0.0).astype(jnp.bfloat16)
    first = part * HALF * OCC
    for k in range(HALF * OCC // CHUNK):
        p = p_ref[first + k * CHUNK:first + (k + 1) * CHUNK, :]
        high = p.astype(jnp.bfloat16)
        low = (p - high.astype(jnp.float32)).astype(jnp.bfloat16)
        flipped = jnp.dot(high, onehot[...], preferred_element_type=jnp.float32)
        flipped = flipped + jnp.dot(low, onehot[...], preferred_element_type=jnp.float32)
        for g in range(8):
            turned[g, k * CHUNK:(k + 1) * CHUNK, :] = flipped[:, g * LANES:(g + 1) * LANES]

    def rows(z, carry):
        for e in range(4):
            i = 8 * lax.rem(y + e, 4) + z
            straight = pl.ds(pl.multiple_of(i * OCC + part * HALF, HALF), HALF)
            slot = pl.ds(pl.multiple_of(z * HALF, HALF), HALF)
            for side, out_ref in ((1 - core, sent_ref), (core, kept_ref)):
                for d in range(4):
                    g = 2 * lax.rem(x + d, 4) + side
                    columns = pl.ds(pl.multiple_of(g * LANES, LANES), LANES)
                    value = p_ref[straight, columns] + turned[g, pl.ds(i, HALF, stride=OCC), :]
                    if part == 0:
                        out_ref[d, e, slot, :] = value
                    else:
                        out_ref[e, d, slot, :] = value
        return carry

    lax.fori_loop(0, 8, rows, 0)


def mirrored(partial, part):
    def kernel(*refs):
        mirror_kernel(part, *refs)

    out = jax.ShapeDtypeStruct((4, 4, 8 * HALF, LANES), jnp.float32)
    return pl.pallas_call(
        kernel,
        out_shape=(out, out),
        scratch_shapes=[
            pltpu.VMEM((PAIRS, PAIRS), jnp.bfloat16),
            pltpu.VMEM((8, HALF * OCC, LANES), jnp.float32),
        ],
        compiler_params=pltpu.CompilerParams(vmem_limit_bytes=24 * 2**20),
        cost_estimate=pl.CostEstimate(flops=2 * PAIRS**3, bytes_accessed=6 * 2**20, transcendentals=0),
        name=f"mirror_{part}",
    )(partial)


def gram_entry(errors, k, l, lane, message):
    value = jnp.sum(errors[k] * errors[l], keepdims=True)
    return jnp.where(lane == HIST * k + l, value, message)


def prepare_kernel(hist_ref, den_ref, errors_ref, following_ref, den_out_ref, message_ref):
    lane = lax.broadcasted_iota(jnp.int32, (8, LANES), 1)
    errors = [hist_ref[k + 1] - hist_ref[k] for k in range(HIST - 1)]
    message = jnp.zeros((8, LANES), jnp.float32)
    for k in range(HIST - 1):
        errors_ref[k] = errors[k]
        following_ref[k] = hist_ref[k + 1]
        for l in range(k + 1):
            message = gram_entry(errors, k, l, lane, message)
    den_out_ref[...] = den_ref[...]
    message_ref[...] = message


def gram_kernel(parts_ref, den_ref, errors_ref, following_ref, early_ref, update_ref, message_ref):
    total = parts_ref[0]
    for s in range(1, 8):
        total = total + parts_ref[s]
    update = total / den_ref[...]
    update_ref[...] = update
    errors = [errors_ref[k] for k in range(HIST - 1)] + [update - following_ref[HIST - 2]]
    lane = lax.broadcasted_iota(jnp.int32, (8, LANES), 1)
    message = early_ref[...]
    for l in range(HIST):
        message = gram_entry(errors, HIST - 1, l, lane, message)
    for s in range(32):
        message_ref[s * 8:(s + 1) * 8, :] = message


def tail_kernel(grams_ref, update_ref, following_ref, out_ref, coef_ref):
    row = jnp.sum(grams_ref[...], axis=0, keepdims=True)
    a = [[row[:, HIST * k + l:HIST * k + l + 1] for l in range(k + 1)] for k in range(HIST)]
    trace = a[0][0]
    for k in range(1, HIST):
        trace = trace + a[k][k]
    ridge = 1e-06 * trace / HIST
    for k in range(HIST):
        a[k][k] = a[k][k] + ridge
    low = [[None] * HIST for _ in range(HIST)]
    inverse = [None] * HIST
    for k in range(HIST):
        pivot = a[k][k]
        for m in range(k):
            pivot = pivot - low[k][m] * low[k][m]
        inverse[k] = 1.0 / jnp.sqrt(pivot)
        for n in range(k + 1, HIST):
            entry = a[n][k]
            for m in range(k):
                entry = entry - low[n][m] * low[k][m]
            low[n][k] = entry * inverse[k]
    half = [None] * HIST
    for k in range(HIST):
        value = jnp.ones((1, 1), jnp.float32)
        for m in range(k):
            value = value - low[k][m] * half[m]
        half[k] = value * inverse[k]
    whole = [None] * HIST
    for k in reversed(range(HIST)):
        value = half[k]
        for m in range(k + 1, HIST):
            value = value - low[m][k] * whole[m]
        whole[k] = value * inverse[k]
    total = whole[0]
    for k in range(1, HIST):
        total = total + whole[k]
    lane = lax.broadcasted_iota(jnp.int32, (1, HIST), 1)
    weights = [whole[k] / total for k in range(HIST)]
    coefficients = jnp.zeros((1, HIST), jnp.float32)
    for k in range(HIST):
        coefficients = jnp.where(lane == k, weights[k], coefficients)
    coef_ref[...] = coefficients
    out = weights[HIST - 1] * update_ref[...]
    for k in range(HIST - 1):
        out = out + weights[k] * following_ref[k]
    out_ref[...] = out


def shift(value, axis, distance):
    return lax.ppermute(value, axis, [(i, (i + distance) % 4) for i in range(4)])


def gathered(pieces, axis):
    arrived = [shift(pieces[d], axis, d) for d in (1, 3, 2)]
    return (pieces[0] + arrived[0]) + (arrived[1] + arrived[2])


def shards(amplitudes, integrals, denominators, history):
    block = jax.ShapeDtypeStruct((OCC, LANES), jnp.float32)
    slabs = jax.ShapeDtypeStruct((HIST - 1, OCC, LANES), jnp.float32)
    errors, following, divisors, early = pl.pallas_call(
        prepare_kernel,
        out_shape=(slabs, slabs, block, jax.ShapeDtypeStruct((8, LANES), jnp.float32)),
        cost_estimate=pl.CostEstimate(flops=2**18, bytes_accessed=2**19, transcendentals=0),
        compiler_params=SMALL,
        name="prepare",
    )(history, denominators)
    partial = lax.dot_general(
        amplitudes,
        integrals,
        (((0,), (0,)), ((), ())),
        precision=lax.Precision.HIGH,
        preferred_element_type=jnp.float32,
    )
    halves = []
    for part, (axis, then) in enumerate((("x", "y"), ("y", "x"))):
        sent, kept = mirrored(partial, part)
        came = lax.ppermute(sent, "core", [(0, 1), (1, 0)])
        half = gathered([kept[d] + came[d] for d in range(4)], axis)
        half = gathered([half[d] for d in range(4)], then)
        halves.append(half.reshape(8, HALF, LANES))
    parts = lax.all_to_all(jnp.concatenate(halves, axis=1), "z", 0, 0, tiled=True)
    update, message = pl.pallas_call(
        gram_kernel,
        out_shape=(block, jax.ShapeDtypeStruct((256, LANES), jnp.float32)),
        compiler_params=SMALL,
        name="gram",
    )(parts, divisors, errors, following, early)
    grams = lax.all_to_all(message, ("x", "core", "y", "z"), 0, 0, tiled=True)
    extrapolated, coefficients = pl.pallas_call(
        tail_kernel,
        out_shape=(block, jax.ShapeDtypeStruct((1, HIST), jnp.float32)),
        compiler_params=SMALL,
        name="tail",
    )(grams, update, following)
    return extrapolated, coefficients.reshape(HIST)


def solution(mesh):
    cores = Mesh(mesh.devices.reshape(4, 2, 4, 8), ("x", "core", "y", "z"))
    pairs = P(("x", "core", "y", "z"), None)
    return jax.shard_map(
        shards,
        mesh=cores,
        in_specs=(pairs, pairs, P(("y", "z"), ("x", "core")), P(None, ("y", "z"), ("x", "core"))),
        out_specs=(P(("y", "z"), ("x", "core")), P()),
        check_vma=False,
    )
```

```python
import jax
import jax.numpy as jnp
from jax import lax
from jax.experimental import pallas as pl
from jax.experimental.pallas import tpu as pltpu
from jax.sharding import Mesh, PartitionSpec as P

OCC = 32
VBLK = 32
PAIRS = 1024
LANES = 128
HIST = 8

SMALL = pltpu.CompilerParams(vmem_limit_bytes=4 * 2**20)


def hot_kernel(hot_ref):
    source = lax.broadcasted_iota(jnp.int32, (PAIRS, LANES), 0)
    lane = lax.broadcasted_iota(jnp.int32, (PAIRS, LANES), 1)
    for g in range(8):
        target = g * LANES + lane
        wanted = (target % VBLK) * VBLK + target // VBLK
        hot_ref[:, g * LANES:(g + 1) * LANES] = jnp.where(source == wanted, 1.0, 0.0).astype(jnp.bfloat16)


def piece_kernel(distance, p_ref, hot_ref, sent_ref, kept_ref, turned):
    group = lax.rem(lax.axis_index("y") + distance, 4)
    core = lax.axis_index("core")
    p = p_ref[:, group].reshape(8 * OCC, PAIRS)
    high = p.astype(jnp.bfloat16)
    low = (p - high.astype(jnp.float32)).astype(jnp.bfloat16)
    flipped = jnp.dot(high, hot_ref[...], preferred_element_type=jnp.float32)
    flipped = flipped + jnp.dot(low, hot_ref[...], preferred_element_type=jnp.float32)
    for g in range(8):
        turned[g] = flipped[:, g * LANES:(g + 1) * LANES]
    for z in range(8):
        i = group * 8 + z
        for side, out_ref in ((1 - core, sent_ref), (core, kept_ref)):
            for x in range(4):
                g = 2 * x + side
                columns = pl.ds(pl.multiple_of(g * LANES, LANES), LANES)
                straight = p_ref[i, :, :, columns].reshape(OCC, LANES)
                out_ref[z, x] = straight + turned[g, pl.ds(z, OCC, stride=8), :]


def piece(partial, hot, distance):
    def kernel(*refs):
        piece_kernel(distance, *refs)

    out = jax.ShapeDtypeStruct((8, 4, OCC, LANES), jnp.float32)
    return pl.pallas_call(
        kernel,
        out_shape=(out, out),
        scratch_shapes=[pltpu.VMEM((8, 8 * OCC, LANES), jnp.float32)],
        compiler_params=pltpu.CompilerParams(vmem_limit_bytes=16 * 2**20),
        cost_estimate=pl.CostEstimate(flops=PAIRS**3, bytes_accessed=5 * 2**20, transcendentals=0),
    )(partial, hot)


def prepare_kernel(own_ref, a_ref, b_ref, c_ref, errors_ref, last_ref, den_ref, following_ref, message_ref):
    x = lax.axis_index("x")
    lane = lax.broadcasted_iota(jnp.int32, (8, LANES), 1)
    sums = {}
    for distance, ref in ((0, own_ref), (1, a_ref), (2, b_ref), (3, c_ref)):
        slot = lax.rem(x - distance + 4, 4)
        errors = [ref[k + 1] - ref[k] for k in range(HIST - 1)]
        for k in range(HIST - 1):
            errors_ref[k, slot] = errors[k]
            for l in range(k + 1):
                product = errors[k] * errors[l]
                sums[k, l] = sums[k, l] + product if (k, l) in sums else product
        last_ref[slot] = ref[HIST - 1]
        den_ref[slot] = ref[HIST]
    for k in range(HIST - 1):
        following_ref[k] = own_ref[k + 1]
    message = jnp.zeros((8, LANES), jnp.float32)
    for k in range(HIST - 1):
        for l in range(k + 1):
            message = jnp.where(lane == HIST * k + l, jnp.sum(sums[k, l], keepdims=True), message)
    message_ref[...] = message


def gram_kernel(own_ref, a_ref, b_ref, c_ref, den_ref, errors_ref, last_ref, early_ref, update_ref, message_ref):
    lane = lax.broadcasted_iota(jnp.int32, (8, LANES), 1)
    sums = [jnp.zeros((OCC, LANES), jnp.float32)] * HIST
    for x in range(4):
        total = (own_ref[x] + a_ref[x]) + (b_ref[x] + c_ref[x])
        update = total / den_ref[x]

        @pl.when(lax.axis_index("x") == x)
        def _():
            update_ref[...] = update

        error = update - last_ref[x]
        for l in range(HIST - 1):
            sums[l] = sums[l] + error * errors_ref[l, x]
        sums[HIST - 1] = sums[HIST - 1] + error * error
    message = early_ref[...]
    for l in range(HIST):
        message = jnp.where(lane == HIST * (HIST - 1) + l, jnp.sum(sums[l], keepdims=True), message)
    for s in range(8):
        message_ref[s * 8:(s + 1) * 8, :] = message


def tail_kernel(grams_ref, update_ref, following_ref, out_ref, coef_ref):
    row = jnp.sum(grams_ref[...], axis=0, keepdims=True)
    a = [[row[:, HIST * k + l:HIST * k + l + 1] for l in range(k + 1)] for k in range(HIST)]
    trace = a[0][0]
    for k in range(1, HIST):
        trace = trace + a[k][k]
    ridge = 1e-06 * trace / HIST
    for k in range(HIST):
        a[k][k] = a[k][k] + ridge
    low = [[None] * HIST for _ in range(HIST)]
    inverse = [None] * HIST
    for k in range(HIST):
        pivot = a[k][k]
        for m in range(k):
            pivot = pivot - low[k][m] * low[k][m]
        inverse[k] = 1.0 / jnp.sqrt(pivot)
        for n in range(k + 1, HIST):
            entry = a[n][k]
            for m in range(k):
                entry = entry - low[n][m] * low[k][m]
            low[n][k] = entry * inverse[k]
    half = [None] * HIST
    for k in range(HIST):
        value = jnp.ones((1, 1), jnp.float32)
        for m in range(k):
            value = value - low[k][m] * half[m]
        half[k] = value * inverse[k]
    whole = [None] * HIST
    for k in reversed(range(HIST)):
        value = half[k]
        for m in range(k + 1, HIST):
            value = value - low[m][k] * whole[m]
        whole[k] = value * inverse[k]
    total = whole[0]
    for k in range(1, HIST):
        total = total + whole[k]
    lane = lax.broadcasted_iota(jnp.int32, (1, HIST), 1)
    weights = [whole[k] / total for k in range(HIST)]
    coefficients = jnp.zeros((1, HIST), jnp.float32)
    for k in range(HIST):
        coefficients = jnp.where(lane == k, weights[k], coefficients)
    coef_ref[...] = coefficients
    out = weights[HIST - 1] * update_ref[...]
    for k in range(HIST - 1):
        out = out + weights[k] * following_ref[k]
    out_ref[...] = out


def shift(value, axis, distance):
    return lax.ppermute(value, axis, [(i, (i + distance) % 4) for i in range(4)])


def step(amplitudes, integrals, denominators, history):
    f32 = jnp.float32
    block = jax.ShapeDtypeStruct((OCC, LANES), f32)
    blocks = jax.ShapeDtypeStruct((4, OCC, LANES), f32)
    hot = pl.pallas_call(
        hot_kernel,
        out_shape=jax.ShapeDtypeStruct((PAIRS, PAIRS), jnp.bfloat16),
        compiler_params=SMALL,
        cost_estimate=pl.CostEstimate(flops=2**20, bytes_accessed=2**21, transcendentals=0),
        name="hot",
    )()
    partial = lax.dot_general(
        amplitudes,
        integrals,
        (((0,), (0,)), ((), ())),
        precision=lax.Precision.HIGH,
        preferred_element_type=f32,
    ).reshape(OCC, 4, 8, PAIRS)
    pieces = {}
    moved = {}
    waiting = []
    for distance in (2, 1, 3, 0):
        sent, kept = piece(partial, hot, distance)
        waiting.append((distance, kept, lax.ppermute(sent, "core", [(0, 1), (1, 0)])))
        if len(waiting) == 2 or distance == 0:
            for earlier, kept, came in waiting[:1] if distance else waiting:
                whole = kept + came
                if earlier == 0:
                    pieces[0] = whole
                else:
                    partial, whole = lax.optimization_barrier((partial, whole))
                    moved[earlier] = shift(whole, "y", earlier)
            waiting = waiting[1:]
    arrived = [moved[d] for d in (2, 1, 3)]
    known = jnp.concatenate([history, denominators[None]], axis=0)
    known, pieces[0] = lax.optimization_barrier((known, pieces[0]))
    others = [shift(known, "x", d) for d in (1, 2, 3)]
    errors, last, divisors, following, early = pl.pallas_call(
        prepare_kernel,
        out_shape=(
            jax.ShapeDtypeStruct((HIST - 1, 4, OCC, LANES), f32),
            blocks,
            blocks,
            jax.ShapeDtypeStruct((HIST - 1, OCC, LANES), f32),
            jax.ShapeDtypeStruct((8, LANES), f32),
        ),
        compiler_params=SMALL,
        cost_estimate=pl.CostEstimate(flops=2**20, bytes_accessed=2**20, transcendentals=0),
        name="prepare",
    )(known, *others)
    rows = (pieces[0] + arrived[0]) + (arrived[1] + arrived[2])
    parts = jnp.sum(lax.all_to_all(rows, "z", 0, 0, tiled=True), axis=0)
    sums = [parts] + [shift(parts, "x", d) for d in (1, 3, 2)]
    update, message = pl.pallas_call(
        gram_kernel,
        out_shape=(block, jax.ShapeDtypeStruct((64, LANES), f32)),
        compiler_params=SMALL,
        name="gram",
    )(*sums, divisors, errors, last, early)
    grams = lax.all_to_all(message, ("core", "y", "z"), 0, 0, tiled=True)
    extrapolated, coefficients = pl.pallas_call(
        tail_kernel,
        out_shape=(block, jax.ShapeDtypeStruct((1, HIST), f32)),
        compiler_params=SMALL,
        name="tail",
    )(grams, update, following)
    return extrapolated, coefficients.reshape(HIST)


def solution(mesh):
    cores = Mesh(mesh.devices.reshape(4, 2, 4, 8), ("x", "core", "y", "z"))
    pairs = P(("x", "core", "y", "z"), None)
    return jax.shard_map(
        step,
        mesh=cores,
        in_specs=(pairs, pairs, P(("y", "z"), ("x", "core")), P(None, ("y", "z"), ("x", "core"))),
        out_specs=(P(("y", "z"), ("x", "core")), P()),
        check_vma=False,
    )
```

```python
import jax
import jax.numpy as jnp
from jax import lax
from jax.experimental import pallas as pl
from jax.experimental.pallas import tpu as pltpu
from jax.sharding import Mesh, PartitionSpec as P

OCC = 32
VBLK = 32
PAIRS = 1024
LANES = 128
HALF = OCC // 2
HIST = 8
CHUNK = 256

SMALL = pltpu.CompilerParams(vmem_limit_bytes=4 * 2**20)


def hot_kernel(hot_ref):
    source = lax.broadcasted_iota(jnp.int32, (PAIRS, LANES), 0)
    lane = lax.broadcasted_iota(jnp.int32, (PAIRS, LANES), 1)
    for g in range(8):
        target = g * LANES + lane
        wanted = (target % VBLK) * VBLK + target // VBLK
        hot_ref[:, g * LANES:(g + 1) * LANES] = jnp.where(source == wanted, 1.0, 0.0).astype(jnp.bfloat16)


def mirror_kernel(part, p_ref, hot_ref, sent_ref, kept_ref, turned):
    x = lax.axis_index("x")
    y = lax.axis_index("y")
    core = lax.axis_index("core")
    for k in range(2):
        rows = part * HALF + k * HALF // 2
        p = p_ref[rows:rows + HALF // 2].reshape(CHUNK, PAIRS)
        high = p.astype(jnp.bfloat16)
        low = (p - high.astype(jnp.float32)).astype(jnp.bfloat16)
        flipped = jnp.dot(high, hot_ref[...], preferred_element_type=jnp.float32)
        flipped = flipped + jnp.dot(low, hot_ref[...], preferred_element_type=jnp.float32)
        for g in range(8):
            turned[g, k * CHUNK:(k + 1) * CHUNK, :] = flipped[:, g * LANES:(g + 1) * LANES]
    js = slice(part * HALF, (part + 1) * HALF)
    for e in range(4):
        for z in range(8):
            i = 8 * lax.rem(y + e, 4) + z
            for side, out_ref in ((1 - core, sent_ref), (core, kept_ref)):
                for d in range(4):
                    g = 2 * lax.rem(x + d, 4) + side
                    columns = pl.ds(pl.multiple_of(g * LANES, LANES), LANES)
                    value = p_ref[i, js, columns] + turned[g, pl.ds(i, HALF, stride=OCC), :]
                    if part == 0:
                        out_ref[d, e, z * HALF:(z + 1) * HALF, :] = value
                    else:
                        out_ref[e, d, z * HALF:(z + 1) * HALF, :] = value


def mirrored(partial, hot, part):
    def kernel(*refs):
        mirror_kernel(part, *refs)

    out = jax.ShapeDtypeStruct((4, 4, 8 * HALF, LANES), jnp.float32)
    return pl.pallas_call(
        kernel,
        out_shape=(out, out),
        scratch_shapes=[pltpu.VMEM((8, HALF * OCC, LANES), jnp.float32)],
        compiler_params=pltpu.CompilerParams(vmem_limit_bytes=16 * 2**20),
        cost_estimate=pl.CostEstimate(flops=2 * PAIRS**3, bytes_accessed=6 * 2**20, transcendentals=0),
        name=f"mirror_{part}",
    )(partial, hot)


def join_kernel(*refs):
    joined_ref = refs[-1]
    for part in range(2):
        own, a, b, c = refs[4 * part:4 * part + 4]
        total = (own[...] + a[...]) + (b[...] + c[...])
        joined_ref[:, part * HALF:(part + 1) * HALF, :] = total.reshape(8, HALF, LANES)


def gram_entry(errors, k, l, lane, message):
    value = jnp.sum(errors[k] * errors[l], keepdims=True)
    return jnp.where(lane == HIST * k + l, value, message)


def prepare_kernel(hist_ref, den_ref, errors_ref, following_ref, den_out_ref, message_ref):
    lane = lax.broadcasted_iota(jnp.int32, (8, LANES), 1)
    errors = [hist_ref[k + 1] - hist_ref[k] for k in range(HIST - 1)]
    message = jnp.zeros((8, LANES), jnp.float32)
    for k in range(HIST - 1):
        errors_ref[k] = errors[k]
        following_ref[k] = hist_ref[k + 1]
        for l in range(k + 1):
            message = gram_entry(errors, k, l, lane, message)
    den_out_ref[...] = den_ref[...]
    message_ref[...] = message


def gram_kernel(parts_ref, den_ref, errors_ref, following_ref, early_ref, update_ref, message_ref):
    total = parts_ref[0]
    for s in range(1, 8):
        total = total + parts_ref[s]
    update = total / den_ref[...]
    update_ref[...] = update
    errors = [errors_ref[k] for k in range(HIST - 1)] + [update - following_ref[HIST - 2]]
    lane = lax.broadcasted_iota(jnp.int32, (8, LANES), 1)
    message = early_ref[...]
    for l in range(HIST):
        message = gram_entry(errors, HIST - 1, l, lane, message)
    for s in range(32):
        message_ref[s * 8:(s + 1) * 8, :] = message


def tail_kernel(grams_ref, update_ref, following_ref, out_ref, coef_ref):
    row = jnp.sum(grams_ref[...], axis=0, keepdims=True)
    spread = (1, LANES)
    a = [[jnp.broadcast_to(row[:, HIST * k + l:HIST * k + l + 1], spread) for l in range(k + 1)] for k in range(HIST)]
    trace = a[0][0]
    for k in range(1, HIST):
        trace = trace + a[k][k]
    ridge = 1e-06 * trace / HIST
    for k in range(HIST):
        a[k][k] = a[k][k] + ridge
    low = [[None] * HIST for _ in range(HIST)]
    inverse = [None] * HIST
    for k in range(HIST):
        pivot = a[k][k]
        for m in range(k):
            pivot = pivot - low[k][m] * low[k][m]
        inverse[k] = 1.0 / jnp.sqrt(pivot)
        for n in range(k + 1, HIST):
            entry = a[n][k]
            for m in range(k):
                entry = entry - low[n][m] * low[k][m]
            low[n][k] = entry * inverse[k]
    half = [None] * HIST
    for k in range(HIST):
        value = jnp.ones(spread, jnp.float32)
        for m in range(k):
            value = value - low[k][m] * half[m]
        half[k] = value * inverse[k]
    whole = [None] * HIST
    for k in reversed(range(HIST)):
        value = half[k]
        for m in range(k + 1, HIST):
            value = value - low[m][k] * whole[m]
        whole[k] = value * inverse[k]
    total = whole[0]
    for k in range(1, HIST):
        total = total + whole[k]
    lane = lax.broadcasted_iota(jnp.int32, spread, 1)
    weights = [whole[k] / total for k in range(HIST)]
    coefficients = jnp.zeros(spread, jnp.float32)
    for k in range(HIST):
        coefficients = jnp.where(lane == k, weights[k], coefficients)
    coef_ref[...] = coefficients[:, :HIST]
    out = weights[HIST - 1] * update_ref[...]
    for k in range(HIST - 1):
        out = out + weights[k] * following_ref[k]
    out_ref[...] = out


def shift(value, axis, distance):
    return lax.ppermute(value, axis, [(i, (i + distance) % 4) for i in range(4)])


def exchanged(pieces, axis):
    return [pieces[0]] + [shift(pieces[d], axis, d) for d in (1, 3, 2)]


def shards(amplitudes, integrals, denominators, history):
    block = jax.ShapeDtypeStruct((OCC, LANES), jnp.float32)
    slabs = jax.ShapeDtypeStruct((HIST - 1, OCC, LANES), jnp.float32)
    errors, following, divisors, early = pl.pallas_call(
        prepare_kernel,
        out_shape=(slabs, slabs, block, jax.ShapeDtypeStruct((8, LANES), jnp.float32)),
        cost_estimate=pl.CostEstimate(flops=2**18, bytes_accessed=2**19, transcendentals=0),
        compiler_params=SMALL,
        name="prepare",
    )(history, denominators)
    hot = pl.pallas_call(
        hot_kernel,
        out_shape=jax.ShapeDtypeStruct((PAIRS, PAIRS), jnp.bfloat16),
        compiler_params=SMALL,
        cost_estimate=pl.CostEstimate(flops=2**20, bytes_accessed=2**21, transcendentals=0),
        name="hot",
    )()
    partial = lax.dot_general(
        amplitudes,
        integrals,
        (((0,), (0,)), ((), ())),
        precision=lax.Precision.HIGH,
        preferred_element_type=jnp.float32,
    ).reshape(OCC, OCC, PAIRS)
    halves = []
    for part, (axis, then) in enumerate((("x", "y"), ("y", "x"))):
        sent, kept = mirrored(partial, hot, part)
        came = lax.ppermute(sent, "core", [(0, 1), (1, 0)])
        own, a, b, c = exchanged([kept[d] + came[d] for d in range(4)], axis)
        half = (own + a) + (b + c)
        halves += exchanged([half[d] for d in range(4)], then)
    rows = pl.pallas_call(
        join_kernel,
        out_shape=jax.ShapeDtypeStruct((8, OCC, LANES), jnp.float32),
        compiler_params=SMALL,
        name="join",
    )(*halves)
    parts = lax.all_to_all(rows, "z", 0, 0, tiled=True)
    update, message = pl.pallas_call(
        gram_kernel,
        out_shape=(block, jax.ShapeDtypeStruct((256, LANES), jnp.float32)),
        compiler_params=SMALL,
        name="gram",
    )(parts, divisors, errors, following, early)
    grams = lax.all_to_all(message, ("x", "core", "y", "z"), 0, 0, tiled=True)
    extrapolated, coefficients = pl.pallas_call(
        tail_kernel,
        out_shape=(block, jax.ShapeDtypeStruct((1, HIST), jnp.float32)),
        compiler_params=SMALL,
        name="tail",
    )(grams, update, following)
    return extrapolated, coefficients.reshape(HIST)


def solution(mesh):
    cores = Mesh(mesh.devices.reshape(4, 2, 4, 8), ("x", "core", "y", "z"))
    pairs = P(("x", "core", "y", "z"), None)
    return jax.shard_map(
        shards,
        mesh=cores,
        in_specs=(pairs, pairs, P(("y", "z"), ("x", "core")), P(None, ("y", "z"), ("x", "core"))),
        out_specs=(P(("y", "z"), ("x", "core")), P()),
        check_vma=False,
    )
```

```python
import jax
import jax.numpy as jnp
from jax import lax
from jax.experimental import pallas as pl
from jax.experimental.pallas import tpu as pltpu
from jax.sharding import Mesh, PartitionSpec as P

OCC = 32
VBLK = 32
PAIRS = 1024
LANES = 128
HIST = 8
CHUNK = 256
PITCH = 40

SMALL = pltpu.CompilerParams(vmem_limit_bytes=4 * 2**20)


def hot_kernel(hot_ref):
    source = lax.broadcasted_iota(jnp.int32, (PAIRS, LANES), 0)
    lane = lax.broadcasted_iota(jnp.int32, (PAIRS, LANES), 1)
    for g in range(8):
        target = g * LANES + lane
        wanted = (target % VBLK) * VBLK + target // VBLK
        hot_ref[:, g * LANES:(g + 1) * LANES] = jnp.where(source == wanted, 1.0, 0.0).astype(jnp.bfloat16)


def piece_kernel(distance, p_ref, hot_ref, sent_ref, kept_ref, turned):
    chip = lax.rem(lax.axis_index("x") + distance, 4)
    core = lax.axis_index("core")
    wanted = hot_ref[:, pl.ds(pl.multiple_of(chip * 2 * LANES, LANES), 2 * LANES)]
    for k in range(PAIRS // CHUNK):
        p = p_ref[k * CHUNK:(k + 1) * CHUNK, :]
        high = p.astype(jnp.bfloat16)
        low = (p - high.astype(jnp.float32)).astype(jnp.bfloat16)
        flipped = jnp.dot(high, wanted, preferred_element_type=jnp.float32)
        flipped = flipped + jnp.dot(low, wanted, preferred_element_type=jnp.float32)
        for m in range(CHUNK // OCC):
            j = k * (CHUNK // OCC) + m
            for side in range(2):
                turned[side, j * PITCH:j * PITCH + OCC, :] = flipped[m * OCC:(m + 1) * OCC, side * LANES:(side + 1) * LANES]
    for side, out_ref in ((1 - core, sent_ref), (core, kept_ref)):
        columns = pl.ds(pl.multiple_of((chip * 2 + side) * LANES, LANES), LANES)
        for i in range(OCC):
            rows = slice(i * OCC, (i + 1) * OCC)
            out_ref[rows, :] = p_ref[rows, columns] + turned[side, pl.ds(i, OCC, stride=PITCH), :]


def piece(partial, hot, distance):
    def kernel(*refs):
        piece_kernel(distance, *refs)

    out = jax.ShapeDtypeStruct((PAIRS, LANES), jnp.float32)
    return pl.pallas_call(
        kernel,
        out_shape=(out, out),
        scratch_shapes=[pltpu.VMEM((2, OCC * PITCH, LANES), jnp.float32)],
        compiler_params=pltpu.CompilerParams(vmem_limit_bytes=16 * 2**20),
        cost_estimate=pl.CostEstimate(flops=PAIRS**3, bytes_accessed=5 * 2**20, transcendentals=0),
    )(partial, hot)


def join_kernel(kept_ref, came_ref, low_below, high_below, low_above, high_above, joined_ref):
    middle = PAIRS // 2
    for part, (below, above) in enumerate(((low_below, low_above), (high_below, high_above))):
        rows = slice(part * middle, (part + 1) * middle)
        joined_ref[rows, :] = (kept_ref[rows, :] + came_ref[rows, :]) + (below[...] + above[...])


def gram_entry(errors, k, l, lane, message):
    value = jnp.sum(errors[k] * errors[l], keepdims=True)
    return jnp.where(lane == HIST * k + l, value, message)


def prepare_kernel(hist_ref, den_ref, errors_ref, following_ref, den_out_ref, message_ref):
    lane = lax.broadcasted_iota(jnp.int32, (8, LANES), 1)
    errors = [hist_ref[k + 1] - hist_ref[k] for k in range(HIST - 1)]
    message = jnp.zeros((8, LANES), jnp.float32)
    for k in range(HIST - 1):
        errors_ref[k] = errors[k]
        following_ref[k] = hist_ref[k + 1]
        for l in range(k + 1):
            message = gram_entry(errors, k, l, lane, message)
    den_out_ref[...] = den_ref[...]
    message_ref[...] = message


def gram_kernel(parts_ref, den_ref, errors_ref, following_ref, early_ref, update_ref, message_ref):
    total = parts_ref[0]
    for s in range(1, 32):
        total = total + parts_ref[s]
    update = total / den_ref[...]
    update_ref[...] = update
    errors = [errors_ref[k] for k in range(HIST - 1)] + [update - following_ref[HIST - 2]]
    lane = lax.broadcasted_iota(jnp.int32, (8, LANES), 1)
    message = early_ref[...]
    for l in range(HIST):
        message = gram_entry(errors, HIST - 1, l, lane, message)
    for s in range(32):
        message_ref[s * 8:(s + 1) * 8, :] = message


def tail_kernel(grams_ref, update_ref, following_ref, out_ref, coef_ref):
    row = jnp.sum(grams_ref[...], axis=0, keepdims=True)
    spread = (1, LANES)
    a = [[jnp.broadcast_to(row[:, HIST * k + l:HIST * k + l + 1], spread) for l in range(k + 1)] for k in range(HIST)]
    trace = a[0][0]
    for k in range(1, HIST):
        trace = trace + a[k][k]
    ridge = 1e-06 * trace / HIST
    for k in range(HIST):
        a[k][k] = a[k][k] + ridge
    low = [[None] * HIST for _ in range(HIST)]
    inverse = [None] * HIST
    for k in range(HIST):
        pivot = a[k][k]
        for m in range(k):
            pivot = pivot - low[k][m] * low[k][m]
        inverse[k] = 1.0 / jnp.sqrt(pivot)
        for n in range(k + 1, HIST):
            entry = a[n][k]
            for m in range(k):
                entry = entry - low[n][m] * low[k][m]
            low[n][k] = entry * inverse[k]
    half = [None] * HIST
    for k in range(HIST):
        value = jnp.ones(spread, jnp.float32)
        for m in range(k):
            value = value - low[k][m] * half[m]
        half[k] = value * inverse[k]
    whole = [None] * HIST
    for k in reversed(range(HIST)):
        value = half[k]
        for m in range(k + 1, HIST):
            value = value - low[m][k] * whole[m]
        whole[k] = value * inverse[k]
    total = whole[0]
    for k in range(1, HIST):
        total = total + whole[k]
    lane = lax.broadcasted_iota(jnp.int32, spread, 1)
    weights = [whole[k] / total for k in range(HIST)]
    coefficients = jnp.zeros(spread, jnp.float32)
    for k in range(HIST):
        coefficients = jnp.where(lane == k, weights[k], coefficients)
    coef_ref[...] = coefficients[:, :HIST]
    out = weights[HIST - 1] * update_ref[...]
    for k in range(HIST - 1):
        out = out + weights[k] * following_ref[k]
    out_ref[...] = out


def shift(value, axis, distance):
    return lax.ppermute(value, axis, [(i, (i + distance) % 4) for i in range(4)])


def step(amplitudes, integrals, denominators, history):
    block = jax.ShapeDtypeStruct((OCC, LANES), jnp.float32)
    slabs = jax.ShapeDtypeStruct((HIST - 1, OCC, LANES), jnp.float32)
    errors, following, divisors, early = pl.pallas_call(
        prepare_kernel,
        out_shape=(slabs, slabs, block, jax.ShapeDtypeStruct((8, LANES), jnp.float32)),
        cost_estimate=pl.CostEstimate(flops=2**18, bytes_accessed=2**19, transcendentals=0),
        compiler_params=SMALL,
        name="prepare",
    )(history, denominators)
    hot = pl.pallas_call(
        hot_kernel,
        out_shape=jax.ShapeDtypeStruct((PAIRS, PAIRS), jnp.bfloat16),
        compiler_params=SMALL,
        cost_estimate=pl.CostEstimate(flops=2**20, bytes_accessed=2**21, transcendentals=0),
        name="hot",
    )()
    partial = lax.dot_general(
        amplitudes,
        integrals,
        (((0,), (0,)), ((), ())),
        precision=lax.Precision.HIGH,
        preferred_element_type=jnp.float32,
    )
    pieces = {}
    for distance in (2, 1, 3, 0):
        sent, kept = piece(partial, hot, distance)
        came = lax.ppermute(sent, "core", [(0, 1), (1, 0)])
        pieces[distance] = (kept, came)
    middle = PAIRS // 2

    def half(part, whole):
        kept, came = whole
        rows = slice(part * middle, (part + 1) * middle)
        return kept[rows] + came[rows]

    def relayed(part, whole, arrived):
        whole, arrived = lax.optimization_barrier((whole, arrived))
        return half(part, whole) + arrived

    from_below = shift(half(0, pieces[2]), "x", 1)
    from_above = shift(half(1, pieces[2]), "x", 3)
    below = [None, shift(half(1, pieces[1]), "x", 1)]
    above = [shift(half(0, pieces[3]), "x", 3), None]
    below[0] = shift(relayed(0, pieces[1], from_below), "x", 1)
    above[1] = shift(relayed(1, pieces[3], from_above), "x", 3)
    rows = pl.pallas_call(
        join_kernel,
        out_shape=jax.ShapeDtypeStruct((PAIRS, LANES), jnp.float32),
        compiler_params=SMALL,
        name="join",
    )(*pieces[0], *below, *above)
    parts = lax.all_to_all(rows, ("y", "z"), 0, 0, tiled=True).reshape(32, OCC, LANES)
    update, message = pl.pallas_call(
        gram_kernel,
        out_shape=(block, jax.ShapeDtypeStruct((256, LANES), jnp.float32)),
        compiler_params=SMALL,
        name="gram",
    )(parts, divisors, errors, following, early)
    grams = lax.all_to_all(message, ("x", "core", "y", "z"), 0, 0, tiled=True)
    extrapolated, coefficients = pl.pallas_call(
        tail_kernel,
        out_shape=(block, jax.ShapeDtypeStruct((1, HIST), jnp.float32)),
        compiler_params=SMALL,
        name="tail",
    )(grams, update, following)
    return extrapolated, coefficients.reshape(HIST)


def solution(mesh):
    cores = Mesh(mesh.devices.reshape(4, 2, 4, 8), ("x", "core", "y", "z"))
    pairs = P(("x", "core", "y", "z"), None)
    return jax.shard_map(
        step,
        mesh=cores,
        in_specs=(pairs, pairs, P(("y", "z"), ("x", "core")), P(None, ("y", "z"), ("x", "core"))),
        out_specs=(P(("y", "z"), ("x", "core")), P()),
        check_vma=False,
    )
```

```python
import jax
import jax.numpy as jnp
from jax import lax
from jax.experimental import pallas as pl
from jax.experimental.pallas import tpu as pltpu
from jax.sharding import Mesh, PartitionSpec as P

OCC = 32
VBLK = 32
PAIRS = 1024
LANES = 128
HALF = OCC // 2
HIST = 8
CHUNK = 256
PITCH = 40

SMALL = pltpu.CompilerParams(vmem_limit_bytes=4 * 2**20)


def hot_kernel(hot_ref):
    source = lax.broadcasted_iota(jnp.int32, (PAIRS, LANES), 0)
    lane = lax.broadcasted_iota(jnp.int32, (PAIRS, LANES), 1)
    for g in range(8):
        target = g * LANES + lane
        wanted = (target % VBLK) * VBLK + target // VBLK
        hot_ref[:, g * LANES:(g + 1) * LANES] = jnp.where(source == wanted, 1.0, 0.0).astype(jnp.bfloat16)


def split(p):
    high = p.astype(jnp.bfloat16)
    return high, (p - high.astype(jnp.float32)).astype(jnp.bfloat16)


def columns(group):
    return pl.ds(pl.multiple_of(group * LANES, LANES), LANES)


def low_kernel(distances, p_ref, hot_ref, sent_ref, kept_ref, turned):
    x = lax.axis_index("x")
    y = lax.axis_index("y")
    core = lax.axis_index("core")
    for k in range(2):
        high, low = split(p_ref[k * CHUNK:(k + 1) * CHUNK, :])
        for n, d in enumerate(distances):
            chip = lax.rem(x + d, 4)
            wanted = hot_ref[:, pl.ds(pl.multiple_of(chip * 2 * LANES, LANES), 2 * LANES)]
            flipped = jnp.dot(high, wanted, preferred_element_type=jnp.float32)
            flipped = flipped + jnp.dot(low, wanted, preferred_element_type=jnp.float32)
            for m in range(8):
                rows = slice((8 * k + m) * PITCH, (8 * k + m) * PITCH + OCC)
                for side in range(2):
                    turned[n, side, rows, :] = flipped[m * OCC:(m + 1) * OCC, side * LANES:(side + 1) * LANES]
    for n, d in enumerate(distances):
        chip = lax.rem(x + d, 4)
        for side, out_ref in ((1 - core, sent_ref), (core, kept_ref)):
            for e in range(4):
                for z in range(8):
                    i = 8 * lax.rem(y + e, 4) + z
                    straight = p_ref[pl.ds(pl.multiple_of(i * OCC, OCC), HALF), columns(2 * chip + side)]
                    slot = slice((8 * e + z) * HALF, (8 * e + z + 1) * HALF)
                    out_ref[n, slot, :] = straight + turned[n, side, pl.ds(i, HALF, stride=PITCH), :]


def high_kernel(distances, p_ref, hot_ref, sent_ref, kept_ref, turned):
    x = lax.axis_index("x")
    y = lax.axis_index("y")
    core = lax.axis_index("core")
    p4_ref = p_ref.reshape(OCC, 4, 8, PAIRS)
    p = [p4_ref[HALF:, lax.rem(y + e, 4)].reshape(LANES, PAIRS) for e in distances]
    high, low = split(jnp.concatenate(p, axis=0))
    flipped = jnp.dot(high, hot_ref[...], preferred_element_type=jnp.float32)
    flipped = flipped + jnp.dot(low, hot_ref[...], preferred_element_type=jnp.float32)
    for n in range(len(distances)):
        for g in range(8):
            turned[n, g] = flipped[n * LANES:(n + 1) * LANES, g * LANES:(g + 1) * LANES]
    for n, e in enumerate(distances):
        for z in range(8):
            i = 8 * lax.rem(y + e, 4) + z
            rows = pl.ds(pl.multiple_of(i * OCC + HALF, HALF), HALF)
            for side, out_ref in ((1 - core, sent_ref), (core, kept_ref)):
                for d in range(4):
                    g = 2 * lax.rem(x + d, 4) + side
                    value = p_ref[rows, columns(g)] + turned[n, g, pl.ds(z, HALF, stride=8), :]
                    out_ref[n, d, z * HALF:(z + 1) * HALF, :] = value


def mirrored(partial, hot, part, distances):
    def kernel(*refs):
        (low_kernel, high_kernel)[part](distances, *refs)

    shape = ((2, OCC * HALF, LANES), (2, 4, 8 * HALF, LANES))[part]
    scratch = ((2, 2, HALF * PITCH, LANES), (2, 8, LANES, LANES))[part]
    out = jax.ShapeDtypeStruct(shape, jnp.float32)
    return pl.pallas_call(
        kernel,
        out_shape=(out, out),
        scratch_shapes=[pltpu.VMEM(scratch, jnp.float32)],
        compiler_params=pltpu.CompilerParams(vmem_limit_bytes=16 * 2**20),
        cost_estimate=pl.CostEstimate(flops=PAIRS**3, bytes_accessed=5 * 2**20, transcendentals=0),
    )(partial, hot)


def join_kernel(*refs):
    joined_ref = refs[-1]
    for part in range(2):
        own, a, b, c = refs[4 * part:4 * part + 4]
        total = (own[...] + a[...]) + (b[...] + c[...])
        joined_ref[:, part * HALF:(part + 1) * HALF, :] = total.reshape(8, HALF, LANES)


def gram_entry(errors, k, l, lane, message):
    value = jnp.sum(errors[k] * errors[l], keepdims=True)
    return jnp.where(lane == HIST * k + l, value, message)


def prepare_kernel(hist_ref, den_ref, errors_ref, following_ref, den_out_ref, message_ref):
    lane = lax.broadcasted_iota(jnp.int32, (8, LANES), 1)
    errors = [hist_ref[k + 1] - hist_ref[k] for k in range(HIST - 1)]
    message = jnp.zeros((8, LANES), jnp.float32)
    for k in range(HIST - 1):
        errors_ref[k] = errors[k]
        following_ref[k] = hist_ref[k + 1]
        for l in range(k + 1):
            message = gram_entry(errors, k, l, lane, message)
    den_out_ref[...] = den_ref[...]
    message_ref[...] = message


def gram_kernel(parts_ref, den_ref, errors_ref, following_ref, early_ref, update_ref, message_ref):
    total = parts_ref[0]
    for s in range(1, 8):
        total = total + parts_ref[s]
    update = total / den_ref[...]
    update_ref[...] = update
    errors = [errors_ref[k] for k in range(HIST - 1)] + [update - following_ref[HIST - 2]]
    lane = lax.broadcasted_iota(jnp.int32, (8, LANES), 1)
    message = early_ref[...]
    for l in range(HIST):
        message = gram_entry(errors, HIST - 1, l, lane, message)
    for s in range(32):
        message_ref[s * 8:(s + 1) * 8, :] = message


def tail_kernel(grams_ref, update_ref, following_ref, out_ref, coef_ref):
    row = jnp.sum(grams_ref[...], axis=0, keepdims=True)
    spread = (1, LANES)
    a = [[jnp.broadcast_to(row[:, HIST * k + l:HIST * k + l + 1], spread) for l in range(k + 1)] for k in range(HIST)]
    trace = a[0][0]
    for k in range(1, HIST):
        trace = trace + a[k][k]
    ridge = 1e-06 * trace / HIST
    for k in range(HIST):
        a[k][k] = a[k][k] + ridge
    low = [[None] * HIST for _ in range(HIST)]
    inverse = [None] * HIST
    for k in range(HIST):
        pivot = a[k][k]
        for m in range(k):
            pivot = pivot - low[k][m] * low[k][m]
        inverse[k] = 1.0 / jnp.sqrt(pivot)
        for n in range(k + 1, HIST):
            entry = a[n][k]
            for m in range(k):
                entry = entry - low[n][m] * low[k][m]
            low[n][k] = entry * inverse[k]
    half = [None] * HIST
    for k in range(HIST):
        value = jnp.ones(spread, jnp.float32)
        for m in range(k):
            value = value - low[k][m] * half[m]
        half[k] = value * inverse[k]
    whole = [None] * HIST
    for k in reversed(range(HIST)):
        value = half[k]
        for m in range(k + 1, HIST):
            value = value - low[m][k] * whole[m]
        whole[k] = value * inverse[k]
    total = whole[0]
    for k in range(1, HIST):
        total = total + whole[k]
    lane = lax.broadcasted_iota(jnp.int32, spread, 1)
    weights = [whole[k] / total for k in range(HIST)]
    coefficients = jnp.zeros(spread, jnp.float32)
    for k in range(HIST):
        coefficients = jnp.where(lane == k, weights[k], coefficients)
    coef_ref[...] = coefficients[:, :HIST]
    out = weights[HIST - 1] * update_ref[...]
    for k in range(HIST - 1):
        out = out + weights[k] * following_ref[k]
    out_ref[...] = out


def shift(value, axis, distance):
    return lax.ppermute(value, axis, [(i, (i + distance) % 4) for i in range(4)])


def step(amplitudes, integrals, denominators, history):
    block = jax.ShapeDtypeStruct((OCC, LANES), jnp.float32)
    slabs = jax.ShapeDtypeStruct((HIST - 1, OCC, LANES), jnp.float32)
    errors, following, divisors, early = pl.pallas_call(
        prepare_kernel,
        out_shape=(slabs, slabs, block, jax.ShapeDtypeStruct((8, LANES), jnp.float32)),
        cost_estimate=pl.CostEstimate(flops=2**18, bytes_accessed=2**19, transcendentals=0),
        compiler_params=SMALL,
        name="prepare",
    )(history, denominators)
    hot = pl.pallas_call(
        hot_kernel,
        out_shape=jax.ShapeDtypeStruct((PAIRS, PAIRS), jnp.bfloat16),
        compiler_params=SMALL,
        cost_estimate=pl.CostEstimate(flops=2**20, bytes_accessed=2**21, transcendentals=0),
        name="hot",
    )()
    partial = lax.dot_general(
        amplitudes,
        integrals,
        (((0,), (0,)), ((), ())),
        precision=lax.Precision.HIGH,
        preferred_element_type=jnp.float32,
    )
    halves = []
    for part, axis in enumerate(("x", "y")):
        moved = {}
        for distances in ((2, 1), (3, 0)):
            sent, kept = mirrored(partial, hot, part, distances)
            came = lax.ppermute(sent, "core", [(0, 1), (1, 0)])
            for n, d in enumerate(distances):
                whole = kept[n] + came[n]
                moved[d] = shift(whole, axis, d) if d else whole
        halves.append((moved[0] + moved[1]) + (moved[3] + moved[2]))
    parts = []
    for part, axis in enumerate(("y", "x")):
        half = halves[part].reshape(4, 8 * HALF, LANES)
        parts += [half[0]] + [shift(half[d], axis, d) for d in (2, 1, 3)]
    rows = pl.pallas_call(
        join_kernel,
        out_shape=jax.ShapeDtypeStruct((8, OCC, LANES), jnp.float32),
        compiler_params=SMALL,
        name="join",
    )(*parts)
    parts = lax.all_to_all(rows, "z", 0, 0, tiled=True)
    update, message = pl.pallas_call(
        gram_kernel,
        out_shape=(block, jax.ShapeDtypeStruct((256, LANES), jnp.float32)),
        compiler_params=SMALL,
        name="gram",
    )(parts, divisors, errors, following, early)
    grams = lax.all_to_all(message, ("x", "core", "y", "z"), 0, 0, tiled=True)
    extrapolated, coefficients = pl.pallas_call(
        tail_kernel,
        out_shape=(block, jax.ShapeDtypeStruct((1, HIST), jnp.float32)),
        compiler_params=SMALL,
        name="tail",
    )(grams, update, following)
    return extrapolated, coefficients.reshape(HIST)


def solution(mesh):
    cores = Mesh(mesh.devices.reshape(4, 2, 4, 8), ("x", "core", "y", "z"))
    pairs = P(("x", "core", "y", "z"), None)
    return jax.shard_map(
        step,
        mesh=cores,
        in_specs=(pairs, pairs, P(("y", "z"), ("x", "core")), P(None, ("y", "z"), ("x", "core"))),
        out_specs=(P(("y", "z"), ("x", "core")), P()),
        check_vma=False,
    )
```

```python
import jax
import jax.numpy as jnp
from jax import lax
from jax.experimental import pallas as pl
from jax.experimental.pallas import tpu as pltpu
from jax.sharding import Mesh, PartitionSpec as P

OCC = 32
VBLK = 32
PAIRS = 1024
LANES = 128
LOW = 24
HIGH = OCC - LOW
HIST = 8
CHUNK = 256
PITCH = 40

SMALL = pltpu.CompilerParams(vmem_limit_bytes=4 * 2**20)


def hot_kernel(hot_ref):
    source = lax.broadcasted_iota(jnp.int32, (PAIRS, LANES), 0)
    lane = lax.broadcasted_iota(jnp.int32, (PAIRS, LANES), 1)
    for g in range(8):
        target = g * LANES + lane
        wanted = (target % VBLK) * VBLK + target // VBLK
        hot_ref[:, g * LANES:(g + 1) * LANES] = jnp.where(source == wanted, 1.0, 0.0).astype(jnp.bfloat16)


def split(p):
    high = p.astype(jnp.bfloat16)
    return high, (p - high.astype(jnp.float32)).astype(jnp.bfloat16)


def columns(group):
    return pl.ds(pl.multiple_of(group * LANES, LANES), LANES)


def turn(p_ref, wanted, turned, first, count):
    groups = wanted.shape[1] // LANES
    for k in range(count // 8):
        high, low = split(p_ref[first * OCC + k * CHUNK:first * OCC + (k + 1) * CHUNK, :])
        flipped = jnp.dot(high, wanted, preferred_element_type=jnp.float32)
        flipped = flipped + jnp.dot(low, wanted, preferred_element_type=jnp.float32)
        for m in range(8):
            rows = slice((8 * k + m) * PITCH, (8 * k + m) * PITCH + OCC)
            for g in range(groups):
                turned[g, rows, :] = flipped[m * OCC:(m + 1) * OCC, g * LANES:(g + 1) * LANES]


def low_kernel(distance, p_ref, hot_ref, sent_ref, kept_ref, turned):
    chip = lax.rem(lax.axis_index("x") + distance, 4)
    y = lax.axis_index("y")
    core = lax.axis_index("core")
    wanted = hot_ref[:, pl.ds(pl.multiple_of(chip * 2 * LANES, LANES), 2 * LANES)]
    turn(p_ref, wanted, turned, 0, LOW)
    for side, out_ref in ((1 - core, sent_ref), (core, kept_ref)):
        for e in range(4):
            for z in range(8):
                i = 8 * lax.rem(y + e, 4) + z
                straight = p_ref[pl.ds(pl.multiple_of(i * OCC, OCC), LOW), columns(2 * chip + side)]
                slot = slice((8 * e + z) * LOW, (8 * e + z + 1) * LOW)
                out_ref[slot, :] = straight + turned[side, pl.ds(i, LOW, stride=PITCH), :]


def high_kernel(p_ref, hot_ref, sent_ref, kept_ref, turned):
    x = lax.axis_index("x")
    y = lax.axis_index("y")
    core = lax.axis_index("core")
    turn(p_ref, hot_ref[...], turned, LOW, HIGH)
    for e in range(4):
        for z in range(8):
            i = 8 * lax.rem(y + e, 4) + z
            rows = pl.ds(pl.multiple_of(i * OCC + LOW, HIGH), HIGH)
            for side, out_ref in ((1 - core, sent_ref), (core, kept_ref)):
                for d in range(4):
                    g = 2 * lax.rem(x + d, 4) + side
                    value = p_ref[rows, columns(g)] + turned[g, pl.ds(i, HIGH, stride=PITCH), :]
                    out_ref[e, d, z * HIGH:(z + 1) * HIGH, :] = value


def mirrored(kernel, shape, scratch, partial, hot):
    out = jax.ShapeDtypeStruct(shape, jnp.float32)
    return pl.pallas_call(
        kernel,
        out_shape=(out, out),
        scratch_shapes=[pltpu.VMEM(scratch, jnp.float32)],
        compiler_params=pltpu.CompilerParams(vmem_limit_bytes=16 * 2**20),
        cost_estimate=pl.CostEstimate(flops=PAIRS**3, bytes_accessed=5 * 2**20, transcendentals=0),
    )(partial, hot)


def low_piece(partial, hot, distance):
    def kernel(*refs):
        low_kernel(distance, *refs)

    return mirrored(kernel, (OCC * LOW, LANES), (2, LOW * PITCH, LANES), partial, hot)


def join_kernel(*refs):
    joined_ref = refs[-1]
    for part, rows in enumerate((slice(0, LOW), slice(LOW, OCC))):
        own, a, b, c = refs[4 * part:4 * part + 4]
        total = (own[...] + a[...]) + (b[...] + c[...])
        joined_ref[:, rows, :] = total.reshape(8, rows.stop - rows.start, LANES)


def gram_entry(errors, k, l, lane, message):
    value = jnp.sum(errors[k] * errors[l], keepdims=True)
    return jnp.where(lane == HIST * k + l, value, message)


def prepare_kernel(hist_ref, den_ref, errors_ref, following_ref, den_out_ref, message_ref):
    lane = lax.broadcasted_iota(jnp.int32, (8, LANES), 1)
    errors = [hist_ref[k + 1] - hist_ref[k] for k in range(HIST - 1)]
    message = jnp.zeros((8, LANES), jnp.float32)
    for k in range(HIST - 1):
        errors_ref[k] = errors[k]
        following_ref[k] = hist_ref[k + 1]
        for l in range(k + 1):
            message = gram_entry(errors, k, l, lane, message)
    den_out_ref[...] = den_ref[...]
    message_ref[...] = message


def gram_kernel(parts_ref, den_ref, errors_ref, following_ref, early_ref, update_ref, message_ref):
    total = parts_ref[0]
    for s in range(1, 8):
        total = total + parts_ref[s]
    update = total / den_ref[...]
    update_ref[...] = update
    errors = [errors_ref[k] for k in range(HIST - 1)] + [update - following_ref[HIST - 2]]
    lane = lax.broadcasted_iota(jnp.int32, (8, LANES), 1)
    message = early_ref[...]
    for l in range(HIST):
        message = gram_entry(errors, HIST - 1, l, lane, message)
    for s in range(32):
        message_ref[s * 8:(s + 1) * 8, :] = message


def tail_kernel(grams_ref, update_ref, following_ref, out_ref, coef_ref):
    row = jnp.sum(grams_ref[...], axis=0, keepdims=True)
    spread = (1, LANES)
    a = [[jnp.broadcast_to(row[:, HIST * k + l:HIST * k + l + 1], spread) for l in range(k + 1)] for k in range(HIST)]
    trace = a[0][0]
    for k in range(1, HIST):
        trace = trace + a[k][k]
    ridge = 1e-06 * trace / HIST
    for k in range(HIST):
        a[k][k] = a[k][k] + ridge
    low = [[None] * HIST for _ in range(HIST)]
    inverse = [None] * HIST
    for k in range(HIST):
        pivot = a[k][k]
        for m in range(k):
            pivot = pivot - low[k][m] * low[k][m]
        inverse[k] = 1.0 / jnp.sqrt(pivot)
        for n in range(k + 1, HIST):
            entry = a[n][k]
            for m in range(k):
                entry = entry - low[n][m] * low[k][m]
            low[n][k] = entry * inverse[k]
    half = [None] * HIST
    for k in range(HIST):
        value = jnp.ones(spread, jnp.float32)
        for m in range(k):
            value = value - low[k][m] * half[m]
        half[k] = value * inverse[k]
    whole = [None] * HIST
    for k in reversed(range(HIST)):
        value = half[k]
        for m in range(k + 1, HIST):
            value = value - low[m][k] * whole[m]
        whole[k] = value * inverse[k]
    total = whole[0]
    for k in range(1, HIST):
        total = total + whole[k]
    lane = lax.broadcasted_iota(jnp.int32, spread, 1)
    weights = [whole[k] / total for k in range(HIST)]
    coefficients = jnp.zeros(spread, jnp.float32)
    for k in range(HIST):
        coefficients = jnp.where(lane == k, weights[k], coefficients)
    coef_ref[...] = coefficients[:, :HIST]
    out = weights[HIST - 1] * update_ref[...]
    for k in range(HIST - 1):
        out = out + weights[k] * following_ref[k]
    out_ref[...] = out


def shift(value, axis, distance):
    return lax.ppermute(value, axis, [(i, (i + distance) % 4) for i in range(4)])


def step(amplitudes, integrals, denominators, history):
    block = jax.ShapeDtypeStruct((OCC, LANES), jnp.float32)
    slabs = jax.ShapeDtypeStruct((HIST - 1, OCC, LANES), jnp.float32)
    errors, following, divisors, early = pl.pallas_call(
        prepare_kernel,
        out_shape=(slabs, slabs, block, jax.ShapeDtypeStruct((8, LANES), jnp.float32)),
        cost_estimate=pl.CostEstimate(flops=2**18, bytes_accessed=2**19, transcendentals=0),
        compiler_params=SMALL,
        name="prepare",
    )(history, denominators)
    hot = pl.pallas_call(
        hot_kernel,
        out_shape=jax.ShapeDtypeStruct((PAIRS, PAIRS), jnp.bfloat16),
        compiler_params=SMALL,
        cost_estimate=pl.CostEstimate(flops=2**20, bytes_accessed=2**21, transcendentals=0),
        name="hot",
    )()
    partial = lax.dot_general(
        amplitudes,
        integrals,
        (((0,), (0,)), ((), ())),
        precision=lax.Precision.HIGH,
        preferred_element_type=jnp.float32,
    )
    pieces = {}
    for distance in (2, 1, 3, 0):
        sent, kept = low_piece(partial, hot, distance)
        came = lax.ppermute(sent, "core", [(0, 1), (1, 0)])
        pieces[distance] = (kept, came)
    middle = OCC * LOW // 2

    def half(part, whole):
        kept, came = whole
        rows = slice(part * middle, (part + 1) * middle)
        return kept[rows] + came[rows]

    def relayed(part, whole, arrived):
        whole, arrived = lax.optimization_barrier((whole, arrived))
        return half(part, whole) + arrived

    from_below = shift(half(0, pieces[2]), "x", 1)
    from_above = shift(half(1, pieces[2]), "x", 3)
    below = [None, shift(half(1, pieces[1]), "x", 1)]
    above = [shift(half(0, pieces[3]), "x", 3), None]
    below[0] = shift(relayed(0, pieces[1], from_below), "x", 1)
    above[1] = shift(relayed(1, pieces[3], from_above), "x", 3)
    lows = []
    for h in range(2):
        lows.append(half(h, pieces[0]) + (below[h] + above[h]))
    sent, kept = mirrored(high_kernel, (4, 4, 8 * HIGH, LANES), (8, HIGH * PITCH, LANES), partial, hot)
    came = lax.ppermute(sent, "core", [(0, 1), (1, 0)])
    high = kept[0] + came[0]
    for e in (2, 1, 3):
        high = high + shift(kept[e] + came[e], "y", e)
    low = [piece for h in range(2) for piece in lows[h].reshape(2, 8 * LOW, LANES)]
    parts = [low[0]] + [shift(low[e], "y", e) for e in (2, 1, 3)]
    parts += [high[0]] + [shift(high[d], "x", d) for d in (2, 1, 3)]
    rows = pl.pallas_call(
        join_kernel,
        out_shape=jax.ShapeDtypeStruct((8, OCC, LANES), jnp.float32),
        compiler_params=SMALL,
        name="join",
    )(*parts)
    parts = lax.all_to_all(rows, "z", 0, 0, tiled=True)
    update, message = pl.pallas_call(
        gram_kernel,
        out_shape=(block, jax.ShapeDtypeStruct((256, LANES), jnp.float32)),
        compiler_params=SMALL,
        name="gram",
    )(parts, divisors, errors, following, early)
    grams = lax.all_to_all(message, ("x", "core", "y", "z"), 0, 0, tiled=True)
    extrapolated, coefficients = pl.pallas_call(
        tail_kernel,
        out_shape=(block, jax.ShapeDtypeStruct((1, HIST), jnp.float32)),
        compiler_params=SMALL,
        name="tail",
    )(grams, update, following)
    return extrapolated, coefficients.reshape(HIST)


def solution(mesh):
    cores = Mesh(mesh.devices.reshape(4, 2, 4, 8), ("x", "core", "y", "z"))
    pairs = P(("x", "core", "y", "z"), None)
    return jax.shard_map(
        step,
        mesh=cores,
        in_specs=(pairs, pairs, P(("y", "z"), ("x", "core")), P(None, ("y", "z"), ("x", "core"))),
        out_specs=(P(("y", "z"), ("x", "core")), P()),
        check_vma=False,
    )
```

```python
import jax
import jax.numpy as jnp
from jax import lax
from jax.experimental import pallas as pl
from jax.experimental.pallas import tpu as pltpu
from jax.sharding import Mesh, PartitionSpec as P

OCC = 32
VBLK = 32
PAIRS = 1024
LANES = 128
LOW = 24
HIGH = OCC - LOW
HIST = 8
CHUNK = 256
PITCH = 40

SMALL = pltpu.CompilerParams(vmem_limit_bytes=4 * 2**20)


def hot_kernel(hot_ref):
    source = lax.broadcasted_iota(jnp.int32, (PAIRS, LANES), 0)
    lane = lax.broadcasted_iota(jnp.int32, (PAIRS, LANES), 1)
    for g in range(8):
        target = g * LANES + lane
        wanted = (target % VBLK) * VBLK + target // VBLK
        hot_ref[:, g * LANES:(g + 1) * LANES] = jnp.where(source == wanted, 1.0, 0.0).astype(jnp.bfloat16)


def split(p):
    high = p.astype(jnp.bfloat16)
    return high, (p - high.astype(jnp.float32)).astype(jnp.bfloat16)


def columns(group):
    return pl.ds(pl.multiple_of(group * LANES, LANES), LANES)


def turn(p_ref, wanted, turned, first, count):
    groups = wanted.shape[1] // LANES
    for k in range(count // 8):
        high, low = split(p_ref[first * OCC + k * CHUNK:first * OCC + (k + 1) * CHUNK, :])
        flipped = jnp.dot(high, wanted, preferred_element_type=jnp.float32)
        flipped = flipped + jnp.dot(low, wanted, preferred_element_type=jnp.float32)
        for m in range(8):
            rows = slice((8 * k + m) * PITCH, (8 * k + m) * PITCH + OCC)
            for g in range(groups):
                turned[g, rows, :] = flipped[m * OCC:(m + 1) * OCC, g * LANES:(g + 1) * LANES]


def low_kernel(distance, p_ref, hot_ref, sent_ref, kept_ref, turned):
    chip = lax.rem(lax.axis_index("x") + distance, 4)
    y = lax.axis_index("y")
    core = lax.axis_index("core")
    wanted = hot_ref[:, pl.ds(pl.multiple_of(chip * 2 * LANES, LANES), 2 * LANES)]
    turn(p_ref, wanted, turned, 0, LOW)
    for side, out_ref in ((1 - core, sent_ref), (core, kept_ref)):
        for e in range(4):
            for z in range(8):
                i = 8 * lax.rem(y + e, 4) + z
                straight = p_ref[pl.ds(pl.multiple_of(i * OCC, OCC), LOW), columns(2 * chip + side)]
                slot = slice((8 * e + z) * LOW, (8 * e + z + 1) * LOW)
                out_ref[slot, :] = straight + turned[side, pl.ds(i, LOW, stride=PITCH), :]


def high_kernel(p_ref, hot_ref, sent_ref, kept_ref, turned):
    x = lax.axis_index("x")
    y = lax.axis_index("y")
    core = lax.axis_index("core")
    turn(p_ref, hot_ref[...], turned, LOW, HIGH)
    for e in range(4):
        for z in range(8):
            i = 8 * lax.rem(y + e, 4) + z
            rows = pl.ds(pl.multiple_of(i * OCC + LOW, HIGH), HIGH)
            for side, out_ref in ((1 - core, sent_ref), (core, kept_ref)):
                for d in range(4):
                    g = 2 * lax.rem(x + d, 4) + side
                    value = p_ref[rows, columns(g)] + turned[g, pl.ds(i, HIGH, stride=PITCH), :]
                    out_ref[e, d, z * HIGH:(z + 1) * HIGH, :] = value


def mirrored(kernel, shape, scratch, partial, hot):
    out = jax.ShapeDtypeStruct(shape, jnp.float32)
    return pl.pallas_call(
        kernel,
        out_shape=(out, out),
        scratch_shapes=[pltpu.VMEM(scratch, jnp.float32)],
        compiler_params=pltpu.CompilerParams(vmem_limit_bytes=16 * 2**20),
        cost_estimate=pl.CostEstimate(flops=PAIRS**3, bytes_accessed=5 * 2**20, transcendentals=0),
    )(partial, hot)


def low_piece(partial, hot, distance):
    def kernel(*refs):
        low_kernel(distance, *refs)

    return mirrored(kernel, (OCC * LOW, LANES), (2, LOW * PITCH, LANES), partial, hot)


def join_kernel(*refs):
    joined_ref = refs[-1]
    for part, rows in enumerate((slice(0, LOW), slice(LOW, OCC))):
        own, a, b, c = refs[4 * part:4 * part + 4]
        total = (own[...] + a[...]) + (b[...] + c[...])
        joined_ref[:, rows, :] = total.reshape(8, rows.stop - rows.start, LANES)


def gram_entry(errors, k, l, lane, message):
    value = jnp.sum(errors[k] * errors[l], keepdims=True)
    return jnp.where(lane == HIST * k + l, value, message)


def prepare_kernel(hist_ref, den_ref, errors_ref, following_ref, den_out_ref, message_ref):
    lane = lax.broadcasted_iota(jnp.int32, (8, LANES), 1)
    errors = [hist_ref[k + 1] - hist_ref[k] for k in range(HIST - 1)]
    message = jnp.zeros((8, LANES), jnp.float32)
    for k in range(HIST - 1):
        errors_ref[k] = errors[k]
        following_ref[k] = hist_ref[k + 1]
        for l in range(k + 1):
            message = gram_entry(errors, k, l, lane, message)
    den_out_ref[...] = den_ref[...]
    message_ref[...] = message


def gram_kernel(parts_ref, den_ref, errors_ref, following_ref, early_ref, update_ref, message_ref):
    total = parts_ref[0]
    for s in range(1, 8):
        total = total + parts_ref[s]
    update = total / den_ref[...]
    update_ref[...] = update
    errors = [errors_ref[k] for k in range(HIST - 1)] + [update - following_ref[HIST - 2]]
    lane = lax.broadcasted_iota(jnp.int32, (8, LANES), 1)
    message = early_ref[...]
    for l in range(HIST):
        message = gram_entry(errors, HIST - 1, l, lane, message)
    for s in range(32):
        message_ref[s * 8:(s + 1) * 8, :] = message


def tail_kernel(grams_ref, update_ref, following_ref, out_ref, coef_ref):
    row = jnp.sum(grams_ref[...], axis=0, keepdims=True)
    spread = (1, LANES)
    a = [[jnp.broadcast_to(row[:, HIST * k + l:HIST * k + l + 1], spread) for l in range(k + 1)] for k in range(HIST)]
    trace = a[0][0]
    for k in range(1, HIST):
        trace = trace + a[k][k]
    ridge = 1e-06 * trace / HIST
    for k in range(HIST):
        a[k][k] = a[k][k] + ridge
    low = [[None] * HIST for _ in range(HIST)]
    inverse = [None] * HIST
    for k in range(HIST):
        pivot = a[k][k]
        for m in range(k):
            pivot = pivot - low[k][m] * low[k][m]
        inverse[k] = 1.0 / jnp.sqrt(pivot)
        for n in range(k + 1, HIST):
            entry = a[n][k]
            for m in range(k):
                entry = entry - low[n][m] * low[k][m]
            low[n][k] = entry * inverse[k]
    half = [None] * HIST
    for k in range(HIST):
        value = jnp.ones(spread, jnp.float32)
        for m in range(k):
            value = value - low[k][m] * half[m]
        half[k] = value * inverse[k]
    whole = [None] * HIST
    for k in reversed(range(HIST)):
        value = half[k]
        for m in range(k + 1, HIST):
            value = value - low[m][k] * whole[m]
        whole[k] = value * inverse[k]
    total = whole[0]
    for k in range(1, HIST):
        total = total + whole[k]
    lane = lax.broadcasted_iota(jnp.int32, spread, 1)
    weights = [whole[k] / total for k in range(HIST)]
    coefficients = jnp.zeros(spread, jnp.float32)
    for k in range(HIST):
        coefficients = jnp.where(lane == k, weights[k], coefficients)
    coef_ref[...] = coefficients[:, :HIST]
    out = weights[HIST - 1] * update_ref[...]
    for k in range(HIST - 1):
        out = out + weights[k] * following_ref[k]
    out_ref[...] = out


def shift(value, axis, distance):
    return lax.ppermute(value, axis, [(i, (i + distance) % 4) for i in range(4)])


def step(amplitudes, integrals, denominators, history):
    block = jax.ShapeDtypeStruct((OCC, LANES), jnp.float32)
    slabs = jax.ShapeDtypeStruct((HIST - 1, OCC, LANES), jnp.float32)
    errors, following, divisors, early = pl.pallas_call(
        prepare_kernel,
        out_shape=(slabs, slabs, block, jax.ShapeDtypeStruct((8, LANES), jnp.float32)),
        cost_estimate=pl.CostEstimate(flops=2**18, bytes_accessed=2**19, transcendentals=0),
        compiler_params=SMALL,
        name="prepare",
    )(history, denominators)
    hot = pl.pallas_call(
        hot_kernel,
        out_shape=jax.ShapeDtypeStruct((PAIRS, PAIRS), jnp.bfloat16),
        compiler_params=SMALL,
        cost_estimate=pl.CostEstimate(flops=2**20, bytes_accessed=2**21, transcendentals=0),
        name="hot",
    )()
    partial = lax.dot_general(
        amplitudes,
        integrals,
        (((0,), (0,)), ((), ())),
        precision=lax.Precision.HIGH,
        preferred_element_type=jnp.float32,
    )
    pieces = {}
    for distance in (2, 1, 3, 0):
        sent, kept = low_piece(partial, hot, distance)
        came = lax.ppermute(sent, "core", [(0, 1), (1, 0)])
        pieces[distance] = (kept, came)
    low = pieces[0][0] + pieces[0][1]
    for d in (2, 1, 3):
        low = low + shift(pieces[d][0] + pieces[d][1], "x", d)
    low = low.reshape(4, 8 * LOW, LANES)
    sent, kept = mirrored(high_kernel, (4, 4, 8 * HIGH, LANES), (8, HIGH * PITCH, LANES), partial, hot)
    came = lax.ppermute(sent, "core", [(0, 1), (1, 0)])
    high = kept[0] + came[0]
    for e in (2, 1, 3):
        high = high + shift(kept[e] + came[e], "y", e)
    quarters = [high[0]]
    for d in (2, 1, 3):
        quarters.append(shift(high[d], "x", d))
    parts = [low[0]]
    for e in (2, 1, 3):
        parts.append(shift(low[e], "y", e))
    parts += quarters
    rows = pl.pallas_call(
        join_kernel,
        out_shape=jax.ShapeDtypeStruct((8, OCC, LANES), jnp.float32),
        compiler_params=SMALL,
        name="join",
    )(*parts)
    parts = lax.all_to_all(rows, "z", 0, 0, tiled=True)
    update, message = pl.pallas_call(
        gram_kernel,
        out_shape=(block, jax.ShapeDtypeStruct((256, LANES), jnp.float32)),
        compiler_params=SMALL,
        name="gram",
    )(parts, divisors, errors, following, early)
    grams = lax.all_to_all(message, ("x", "core", "y", "z"), 0, 0, tiled=True)
    extrapolated, coefficients = pl.pallas_call(
        tail_kernel,
        out_shape=(block, jax.ShapeDtypeStruct((1, HIST), jnp.float32)),
        compiler_params=SMALL,
        name="tail",
    )(grams, update, following)
    return extrapolated, coefficients.reshape(HIST)


def solution(mesh):
    cores = Mesh(mesh.devices.reshape(4, 2, 4, 8), ("x", "core", "y", "z"))
    pairs = P(("x", "core", "y", "z"), None)
    return jax.shard_map(
        step,
        mesh=cores,
        in_specs=(pairs, pairs, P(("y", "z"), ("x", "core")), P(None, ("y", "z"), ("x", "core"))),
        out_specs=(P(("y", "z"), ("x", "core")), P()),
        check_vma=False,
    )
```

```python
import jax
import jax.numpy as jnp
from jax import lax
from jax.experimental import pallas as pl
from jax.experimental.pallas import tpu as pltpu
from jax.sharding import Mesh, PartitionSpec as P

OCC = 32
VBLK = 32
PAIRS = 1024
LANES = 128
LOW = 24
HIGH = OCC - LOW
HIST = 8
CHUNK = 256
PITCH = 40

SMALL = pltpu.CompilerParams(vmem_limit_bytes=4 * 2**20)


def hot_kernel(hot_ref):
    source = lax.broadcasted_iota(jnp.int32, (PAIRS, LANES), 0)
    lane = lax.broadcasted_iota(jnp.int32, (PAIRS, LANES), 1)
    for g in range(8):
        target = g * LANES + lane
        wanted = (target % VBLK) * VBLK + target // VBLK
        hot_ref[:, g * LANES:(g + 1) * LANES] = jnp.where(source == wanted, 1.0, 0.0).astype(jnp.bfloat16)


def split(p):
    high = p.astype(jnp.bfloat16)
    return high, (p - high.astype(jnp.float32)).astype(jnp.bfloat16)


def columns(group):
    return pl.ds(pl.multiple_of(group * LANES, LANES), LANES)


def turn(p_ref, wanted, turned, first, count):
    groups = wanted.shape[1] // LANES
    for k in range(count // 8):
        high, low = split(p_ref[first * OCC + k * CHUNK:first * OCC + (k + 1) * CHUNK, :])
        flipped = jnp.dot(high, wanted, preferred_element_type=jnp.float32)
        flipped = flipped + jnp.dot(low, wanted, preferred_element_type=jnp.float32)
        for m in range(8):
            rows = slice((8 * k + m) * PITCH, (8 * k + m) * PITCH + OCC)
            for g in range(groups):
                turned[g, rows, :] = flipped[m * OCC:(m + 1) * OCC, g * LANES:(g + 1) * LANES]


def low_kernel(distance, p_ref, hot_ref, sent_ref, kept_ref, turned):
    chip = lax.rem(lax.axis_index("x") + distance, 4)
    y = lax.axis_index("y")
    core = lax.axis_index("core")
    wanted = hot_ref[:, pl.ds(pl.multiple_of(chip * 2 * LANES, LANES), 2 * LANES)]
    turn(p_ref, wanted, turned, 0, LOW)
    for side, out_ref in ((1 - core, sent_ref), (core, kept_ref)):
        for e in range(4):
            for z in range(8):
                i = 8 * lax.rem(y + e, 4) + z
                straight = p_ref[pl.ds(pl.multiple_of(i * OCC, OCC), LOW), columns(2 * chip + side)]
                slot = slice((8 * e + z) * LOW, (8 * e + z + 1) * LOW)
                out_ref[slot, :] = straight + turned[side, pl.ds(i, LOW, stride=PITCH), :]


def high_kernel(p_ref, hot_ref, sent_ref, kept_ref, turned):
    x = lax.axis_index("x")
    y = lax.axis_index("y")
    core = lax.axis_index("core")
    turn(p_ref, hot_ref[...], turned, LOW, HIGH)
    for e in range(4):
        for z in range(8):
            i = 8 * lax.rem(y + e, 4) + z
            rows = pl.ds(pl.multiple_of(i * OCC + LOW, HIGH), HIGH)
            for side, out_ref in ((1 - core, sent_ref), (core, kept_ref)):
                for d in range(4):
                    g = 2 * lax.rem(x + d, 4) + side
                    value = p_ref[rows, columns(g)] + turned[g, pl.ds(i, HIGH, stride=PITCH), :]
                    out_ref[e, d, z * HIGH:(z + 1) * HIGH, :] = value


def mirrored(kernel, shape, scratch, partial, hot):
    out = jax.ShapeDtypeStruct(shape, jnp.float32)
    return pl.pallas_call(
        kernel,
        out_shape=(out, out),
        scratch_shapes=[pltpu.VMEM(scratch, jnp.float32)],
        compiler_params=pltpu.CompilerParams(vmem_limit_bytes=16 * 2**20),
        cost_estimate=pl.CostEstimate(flops=PAIRS**3, bytes_accessed=5 * 2**20, transcendentals=0),
    )(partial, hot)


def low_piece(partial, hot, distance):
    def kernel(*refs):
        low_kernel(distance, *refs)

    return mirrored(kernel, (OCC * LOW, LANES), (2, LOW * PITCH, LANES), partial, hot)


def join_kernel(*refs):
    joined_ref = refs[-1]
    for part, rows in enumerate((slice(0, LOW), slice(LOW, OCC))):
        own, a, b, c = refs[4 * part:4 * part + 4]
        total = (own[...] + a[...]) + (b[...] + c[...])
        joined_ref[:, rows, :] = total.reshape(8, rows.stop - rows.start, LANES)


def gram_entry(errors, k, l, lane, message):
    value = jnp.sum(errors[k] * errors[l], keepdims=True)
    return jnp.where(lane == HIST * k + l, value, message)


def prepare_kernel(hist_ref, den_ref, errors_ref, following_ref, den_out_ref, message_ref):
    lane = lax.broadcasted_iota(jnp.int32, (8, LANES), 1)
    errors = [hist_ref[k + 1] - hist_ref[k] for k in range(HIST - 1)]
    message = jnp.zeros((8, LANES), jnp.float32)
    for k in range(HIST - 1):
        errors_ref[k] = errors[k]
        following_ref[k] = hist_ref[k + 1]
        for l in range(k + 1):
            message = gram_entry(errors, k, l, lane, message)
    den_out_ref[...] = den_ref[...]
    message_ref[...] = message


def gram_kernel(parts_ref, den_ref, errors_ref, following_ref, early_ref, update_ref, message_ref):
    total = parts_ref[0]
    for s in range(1, 8):
        total = total + parts_ref[s]
    update = total / den_ref[...]
    update_ref[...] = update
    errors = [errors_ref[k] for k in range(HIST - 1)] + [update - following_ref[HIST - 2]]
    lane = lax.broadcasted_iota(jnp.int32, (8, LANES), 1)
    message = early_ref[...]
    for l in range(HIST):
        message = gram_entry(errors, HIST - 1, l, lane, message)
    message_ref[...] = message


def tail_kernel(grams_ref, update_ref, following_ref, out_ref, coef_ref):
    row = jnp.sum(grams_ref[...], axis=0, keepdims=True)
    spread = (1, LANES)
    a = [[jnp.broadcast_to(row[:, HIST * k + l:HIST * k + l + 1], spread) for l in range(k + 1)] for k in range(HIST)]
    trace = a[0][0]
    for k in range(1, HIST):
        trace = trace + a[k][k]
    ridge = 1e-06 * trace / HIST
    for k in range(HIST):
        a[k][k] = a[k][k] + ridge
    low = [[None] * HIST for _ in range(HIST)]
    inverse = [None] * HIST
    for k in range(HIST):
        pivot = a[k][k]
        for m in range(k):
            pivot = pivot - low[k][m] * low[k][m]
        inverse[k] = 1.0 / jnp.sqrt(pivot)
        for n in range(k + 1, HIST):
            entry = a[n][k]
            for m in range(k):
                entry = entry - low[n][m] * low[k][m]
            low[n][k] = entry * inverse[k]
    half = [None] * HIST
    for k in range(HIST):
        value = jnp.ones(spread, jnp.float32)
        for m in range(k):
            value = value - low[k][m] * half[m]
        half[k] = value * inverse[k]
    whole = [None] * HIST
    for k in reversed(range(HIST)):
        value = half[k]
        for m in range(k + 1, HIST):
            value = value - low[m][k] * whole[m]
        whole[k] = value * inverse[k]
    total = whole[0]
    for k in range(1, HIST):
        total = total + whole[k]
    lane = lax.broadcasted_iota(jnp.int32, spread, 1)
    weights = [whole[k] / total for k in range(HIST)]
    coefficients = jnp.zeros(spread, jnp.float32)
    for k in range(HIST):
        coefficients = jnp.where(lane == k, weights[k], coefficients)
    coef_ref[...] = coefficients[:, :HIST]
    out = weights[HIST - 1] * update_ref[...]
    for k in range(HIST - 1):
        out = out + weights[k] * following_ref[k]
    out_ref[...] = out


def shift(value, axis, distance):
    return lax.ppermute(value, axis, [(i, (i + distance) % 4) for i in range(4)])


def product(a, b):
    return lax.dot_general(
        a,
        b,
        (((0,), (0,)), ((), ())),
        precision=lax.Precision.HIGH,
        preferred_element_type=jnp.float32,
    )


def step(amplitudes, integrals, denominators, history):
    block = jax.ShapeDtypeStruct((OCC, LANES), jnp.float32)
    slabs = jax.ShapeDtypeStruct((HIST - 1, OCC, LANES), jnp.float32)
    errors, following, divisors, early = pl.pallas_call(
        prepare_kernel,
        out_shape=(slabs, slabs, block, jax.ShapeDtypeStruct((8, LANES), jnp.float32)),
        cost_estimate=pl.CostEstimate(flops=2**18, bytes_accessed=2**19, transcendentals=0),
        compiler_params=SMALL,
        name="prepare",
    )(history, denominators)
    hot = pl.pallas_call(
        hot_kernel,
        out_shape=jax.ShapeDtypeStruct((PAIRS, PAIRS), jnp.bfloat16),
        compiler_params=SMALL,
        cost_estimate=pl.CostEstimate(flops=2**20, bytes_accessed=2**21, transcendentals=0),
        name="hot",
    )()
    partial = product(amplitudes[:PAIRS // 2], integrals[:PAIRS // 2])
    partial = partial + product(amplitudes[PAIRS // 2:], integrals[PAIRS // 2:])
    pieces = {}
    for distance in (2, 1, 3, 0):
        sent, kept = low_piece(partial, hot, distance)
        came = lax.ppermute(sent, "core", [(0, 1), (1, 0)])
        pieces[distance] = (kept, came)
    low = pieces[0][0] + pieces[0][1]
    for d in (2, 1, 3):
        low = low + shift(pieces[d][0] + pieces[d][1], "x", d)
    low = low.reshape(4, 8 * LOW, LANES)
    sent, kept = mirrored(high_kernel, (4, 4, 8 * HIGH, LANES), (8, HIGH * PITCH, LANES), partial, hot)
    came = lax.ppermute(sent, "core", [(0, 1), (1, 0)])
    high = kept[0] + came[0]
    for e in (2, 1, 3):
        high = high + shift(kept[e] + came[e], "y", e)
    quarters = [high[0]]
    for d in (2, 1, 3):
        quarters.append(shift(high[d], "x", d))
    parts = [low[0]]
    for e in (2, 1, 3):
        parts.append(shift(low[e], "y", e))
    parts += quarters
    rows = pl.pallas_call(
        join_kernel,
        out_shape=jax.ShapeDtypeStruct((8, OCC, LANES), jnp.float32),
        compiler_params=SMALL,
        name="join",
    )(*parts)
    parts = lax.all_to_all(rows, "z", 0, 0, tiled=True)
    update, message = pl.pallas_call(
        gram_kernel,
        out_shape=(block, jax.ShapeDtypeStruct((8, LANES), jnp.float32)),
        compiler_params=SMALL,
        name="gram",
    )(parts, divisors, errors, following, early)
    message = message + lax.ppermute(message, "core", [(0, 1), (1, 0)])
    message = jnp.broadcast_to(message, (16, 8, LANES)).reshape(16 * 8, LANES)
    grams = lax.all_to_all(message, ("x", "y", "z"), 0, 0, tiled=True)
    extrapolated, coefficients = pl.pallas_call(
        tail_kernel,
        out_shape=(block, jax.ShapeDtypeStruct((1, HIST), jnp.float32)),
        compiler_params=SMALL,
        name="tail",
    )(grams, update, following)
    return extrapolated, coefficients.reshape(HIST)


def solution(mesh):
    cores = Mesh(mesh.devices.reshape(4, 2, 4, 8), ("x", "core", "y", "z"))
    pairs = P(("x", "core", "y", "z"), None)
    return jax.shard_map(
        step,
        mesh=cores,
        in_specs=(pairs, pairs, P(("y", "z"), ("x", "core")), P(None, ("y", "z"), ("x", "core"))),
        out_specs=(P(("y", "z"), ("x", "core")), P()),
        check_vma=False,
    )
```

```python
import jax
import jax.numpy as jnp
from jax import lax
from jax.experimental import pallas as pl
from jax.experimental.pallas import tpu as pltpu
from jax.sharding import Mesh, PartitionSpec as P

OCC = 32
VBLK = 32
PAIRS = 1024
LANES = 128
LOW = 24
HIGH = OCC - LOW
HIST = 8
CHUNK = 256
PITCH = 40

SMALL = pltpu.CompilerParams(vmem_limit_bytes=4 * 2**20)


def hot_kernel(hot_ref):
    source = lax.broadcasted_iota(jnp.int32, (PAIRS, LANES), 0)
    lane = lax.broadcasted_iota(jnp.int32, (PAIRS, LANES), 1)
    for g in range(8):
        target = g * LANES + lane
        wanted = (target % VBLK) * VBLK + target // VBLK
        hot_ref[:, g * LANES:(g + 1) * LANES] = jnp.where(source == wanted, 1.0, 0.0).astype(jnp.bfloat16)


def split(p):
    high = p.astype(jnp.bfloat16)
    return high, (p - high.astype(jnp.float32)).astype(jnp.bfloat16)


def columns(group):
    return pl.ds(pl.multiple_of(group * LANES, LANES), LANES)


def turn(p_ref, wanted, turned, first, count):
    groups = wanted.shape[1] // LANES
    for k in range(count // 8):
        high, low = split(p_ref[first * OCC + k * CHUNK:first * OCC + (k + 1) * CHUNK, :])
        flipped = jnp.dot(high, wanted, preferred_element_type=jnp.float32)
        flipped = flipped + jnp.dot(low, wanted, preferred_element_type=jnp.float32)
        for m in range(8):
            rows = slice((8 * k + m) * PITCH, (8 * k + m) * PITCH + OCC)
            for g in range(groups):
                turned[g, rows, :] = flipped[m * OCC:(m + 1) * OCC, g * LANES:(g + 1) * LANES]


def low_kernel(distance, p_ref, hot_ref, sent_ref, kept_ref, turned):
    chip = lax.rem(lax.axis_index("x") + distance, 4)
    y = lax.axis_index("y")
    core = lax.axis_index("core")
    wanted = hot_ref[:, pl.ds(pl.multiple_of(chip * 2 * LANES, LANES), 2 * LANES)]
    turn(p_ref, wanted, turned, 0, LOW)
    for side, out_ref in ((1 - core, sent_ref), (core, kept_ref)):
        for e in range(4):
            for z in range(8):
                i = 8 * lax.rem(y + e, 4) + z
                straight = p_ref[pl.ds(pl.multiple_of(i * OCC, OCC), LOW), columns(2 * chip + side)]
                slot = slice((8 * e + z) * LOW, (8 * e + z + 1) * LOW)
                out_ref[slot, :] = straight + turned[side, pl.ds(i, LOW, stride=PITCH), :]


def high_kernel(p_ref, hot_ref, sent_ref, kept_ref, turned):
    x = lax.axis_index("x")
    y = lax.axis_index("y")
    core = lax.axis_index("core")
    turn(p_ref, hot_ref[...], turned, LOW, HIGH)
    for e in range(4):
        for z in range(8):
            i = 8 * lax.rem(y + e, 4) + z
            rows = pl.ds(pl.multiple_of(i * OCC + LOW, HIGH), HIGH)
            for side, out_ref in ((1 - core, sent_ref), (core, kept_ref)):
                for d in range(4):
                    g = 2 * lax.rem(x + d, 4) + side
                    value = p_ref[rows, columns(g)] + turned[g, pl.ds(i, HIGH, stride=PITCH), :]
                    out_ref[e, d, z * HIGH:(z + 1) * HIGH, :] = value


def mirrored(kernel, shape, scratch, partial, hot):
    out = jax.ShapeDtypeStruct(shape, jnp.float32)
    return pl.pallas_call(
        kernel,
        out_shape=(out, out),
        scratch_shapes=[pltpu.VMEM(scratch, jnp.float32)],
        compiler_params=pltpu.CompilerParams(vmem_limit_bytes=16 * 2**20),
        cost_estimate=pl.CostEstimate(flops=PAIRS**3, bytes_accessed=5 * 2**20, transcendentals=0),
    )(partial, hot)


def low_piece(partial, hot, distance):
    def kernel(*refs):
        low_kernel(distance, *refs)

    return mirrored(kernel, (OCC * LOW, LANES), (2, LOW * PITCH, LANES), partial, hot)


def join_kernel(*refs):
    joined_ref = refs[-1]
    for part, rows in enumerate((slice(0, LOW), slice(LOW, OCC))):
        own, a, b, c = refs[4 * part:4 * part + 4]
        total = (own[...] + a[...]) + (b[...] + c[...])
        joined_ref[:, rows, :] = total.reshape(8, rows.stop - rows.start, LANES)


def gram_entry(errors, k, l, lane, message):
    value = jnp.sum(errors[k] * errors[l], keepdims=True)
    return jnp.where(lane == HIST * k + l, value, message)


def prepare_kernel(hist_ref, den_ref, errors_ref, following_ref, den_out_ref, message_ref):
    lane = lax.broadcasted_iota(jnp.int32, (8, LANES), 1)
    errors = [hist_ref[k + 1] - hist_ref[k] for k in range(HIST - 1)]
    message = jnp.zeros((8, LANES), jnp.float32)
    for k in range(HIST - 1):
        errors_ref[k] = errors[k]
        following_ref[k] = hist_ref[k + 1]
        for l in range(k + 1):
            message = gram_entry(errors, k, l, lane, message)
    den_out_ref[...] = den_ref[...]
    message_ref[...] = message


def gram_kernel(parts_ref, den_ref, errors_ref, following_ref, early_ref, update_ref, message_ref):
    total = parts_ref[0]
    for s in range(1, 8):
        total = total + parts_ref[s]
    update = total / den_ref[...]
    update_ref[...] = update
    errors = [errors_ref[k] for k in range(HIST - 1)] + [update - following_ref[HIST - 2]]
    lane = lax.broadcasted_iota(jnp.int32, (8, LANES), 1)
    message = early_ref[...]
    for l in range(HIST):
        message = gram_entry(errors, HIST - 1, l, lane, message)
    for s in range(32):
        message_ref[s * 8:(s + 1) * 8, :] = message


def tail_kernel(grams_ref, update_ref, following_ref, out_ref, coef_ref):
    row = jnp.sum(grams_ref[...], axis=0, keepdims=True)
    spread = (1, LANES)
    a = [[jnp.broadcast_to(row[:, HIST * k + l:HIST * k + l + 1], spread) for l in range(k + 1)] for k in range(HIST)]
    trace = a[0][0]
    for k in range(1, HIST):
        trace = trace + a[k][k]
    ridge = 1e-06 * trace / HIST
    for k in range(HIST):
        a[k][k] = a[k][k] + ridge
    low = [[None] * HIST for _ in range(HIST)]
    inverse = [None] * HIST
    for k in range(HIST):
        pivot = a[k][k]
        for m in range(k):
            pivot = pivot - low[k][m] * low[k][m]
        inverse[k] = 1.0 / jnp.sqrt(pivot)
        for n in range(k + 1, HIST):
            entry = a[n][k]
            for m in range(k):
                entry = entry - low[n][m] * low[k][m]
            low[n][k] = entry * inverse[k]
    half = [None] * HIST
    for k in range(HIST):
        value = jnp.ones(spread, jnp.float32)
        for m in range(k):
            value = value - low[k][m] * half[m]
        half[k] = value * inverse[k]
    whole = [None] * HIST
    for k in reversed(range(HIST)):
        value = half[k]
        for m in range(k + 1, HIST):
            value = value - low[m][k] * whole[m]
        whole[k] = value * inverse[k]
    total = whole[0]
    for k in range(1, HIST):
        total = total + whole[k]
    lane = lax.broadcasted_iota(jnp.int32, spread, 1)
    weights = [whole[k] / total for k in range(HIST)]
    coefficients = jnp.zeros(spread, jnp.float32)
    for k in range(HIST):
        coefficients = jnp.where(lane == k, weights[k], coefficients)
    coef_ref[...] = coefficients[:, :HIST]
    out = weights[HIST - 1] * update_ref[...]
    for k in range(HIST - 1):
        out = out + weights[k] * following_ref[k]
    out_ref[...] = out


def shift(value, axis, distance):
    return lax.ppermute(value, axis, [(i, (i + distance) % 4) for i in range(4)])


def product(a, b):
    return lax.dot_general(
        a,
        b,
        (((0,), (0,)), ((), ())),
        precision=lax.Precision.HIGH,
        preferred_element_type=jnp.float32,
    )


def step(amplitudes, integrals, denominators, history):
    block = jax.ShapeDtypeStruct((OCC, LANES), jnp.float32)
    slabs = jax.ShapeDtypeStruct((HIST - 1, OCC, LANES), jnp.float32)
    errors, following, divisors, early = pl.pallas_call(
        prepare_kernel,
        out_shape=(slabs, slabs, block, jax.ShapeDtypeStruct((8, LANES), jnp.float32)),
        cost_estimate=pl.CostEstimate(flops=2**18, bytes_accessed=2**19, transcendentals=0),
        compiler_params=SMALL,
        name="prepare",
    )(history, denominators)
    hot = pl.pallas_call(
        hot_kernel,
        out_shape=jax.ShapeDtypeStruct((PAIRS, PAIRS), jnp.bfloat16),
        compiler_params=SMALL,
        cost_estimate=pl.CostEstimate(flops=2**20, bytes_accessed=2**21, transcendentals=0),
        name="hot",
    )()
    partial = product(amplitudes[:PAIRS // 2], integrals[:PAIRS // 2])
    partial = partial + product(amplitudes[PAIRS // 2:], integrals[PAIRS // 2:])
    pieces = {}
    for distance in (2, 1, 3, 0):
        sent, kept = low_piece(partial, hot, distance)
        came = lax.ppermute(sent, "core", [(0, 1), (1, 0)])
        pieces[distance] = (kept, came)
    middle = OCC * LOW // 2

    def half(part, whole):
        kept, came = whole
        rows = slice(part * middle, (part + 1) * middle)
        return kept[rows] + came[rows]

    def relayed(part, whole, arrived):
        whole, arrived = lax.optimization_barrier((whole, arrived))
        return half(part, whole) + arrived

    from_below = shift(half(0, pieces[2]), "x", 1)
    from_above = shift(half(1, pieces[2]), "x", 3)
    below = [None, shift(half(1, pieces[1]), "x", 1)]
    above = [shift(half(0, pieces[3]), "x", 3), None]
    below[0] = shift(relayed(0, pieces[1], from_below), "x", 1)
    above[1] = shift(relayed(1, pieces[3], from_above), "x", 3)
    lows = []
    for h in range(2):
        lows.append(half(h, pieces[0]) + (below[h] + above[h]))
    sent, kept = mirrored(high_kernel, (4, 4, 8 * HIGH, LANES), (8, HIGH * PITCH, LANES), partial, hot)
    came = lax.ppermute(sent, "core", [(0, 1), (1, 0)])
    high = kept[0] + came[0]
    for e in (2, 1, 3):
        high = high + shift(kept[e] + came[e], "y", e)
    low = [piece for h in range(2) for piece in lows[h].reshape(2, 8 * LOW, LANES)]
    quarters = [high[0]]
    for d in (2, 1, 3):
        quarters.append(shift(high[d], "x", d))
    parts = [low[0]]
    for e in (2, 1, 3):
        parts.append(shift(low[e], "y", e))
    parts += quarters
    rows = pl.pallas_call(
        join_kernel,
        out_shape=jax.ShapeDtypeStruct((8, OCC, LANES), jnp.float32),
        compiler_params=SMALL,
        name="join",
    )(*parts)
    parts = lax.all_to_all(rows, "z", 0, 0, tiled=True)
    update, message = pl.pallas_call(
        gram_kernel,
        out_shape=(block, jax.ShapeDtypeStruct((256, LANES), jnp.float32)),
        compiler_params=SMALL,
        name="gram",
    )(parts, divisors, errors, following, early)
    grams = lax.all_to_all(message, ("x", "core", "y", "z"), 0, 0, tiled=True)
    extrapolated, coefficients = pl.pallas_call(
        tail_kernel,
        out_shape=(block, jax.ShapeDtypeStruct((1, HIST), jnp.float32)),
        compiler_params=SMALL,
        name="tail",
    )(grams, update, following)
    return extrapolated, coefficients.reshape(HIST)


def solution(mesh):
    cores = Mesh(mesh.devices.reshape(4, 2, 4, 8), ("x", "core", "y", "z"))
    pairs = P(("x", "core", "y", "z"), None)
    return jax.shard_map(
        step,
        mesh=cores,
        in_specs=(pairs, pairs, P(("y", "z"), ("x", "core")), P(None, ("y", "z"), ("x", "core"))),
        out_specs=(P(("y", "z"), ("x", "core")), P()),
        check_vma=False,
    )
```

```python
import jax
import jax.numpy as jnp
from jax import lax
from jax.experimental import pallas as pl
from jax.experimental.pallas import tpu as pltpu
from jax.sharding import Mesh, PartitionSpec as P

OCC = 32
VBLK = 32
PAIRS = 1024
LANES = 128
LOW = 24
HIGH = OCC - LOW
HIST = 8
CHUNK = 256
PITCH = 40

SMALL = pltpu.CompilerParams(vmem_limit_bytes=4 * 2**20)


def hot_kernel(hot_ref):
    source = lax.broadcasted_iota(jnp.int32, (PAIRS, LANES), 0)
    lane = lax.broadcasted_iota(jnp.int32, (PAIRS, LANES), 1)
    for g in range(8):
        target = g * LANES + lane
        wanted = (target % VBLK) * VBLK + target // VBLK
        hot_ref[:, g * LANES:(g + 1) * LANES] = jnp.where(source == wanted, 1.0, 0.0).astype(jnp.bfloat16)


def split(p):
    high = p.astype(jnp.bfloat16)
    return high, (p - high.astype(jnp.float32)).astype(jnp.bfloat16)


def columns(group):
    return pl.ds(pl.multiple_of(group * LANES, LANES), LANES)


def turn(p_ref, wanted, turned, first, count):
    groups = wanted.shape[1] // LANES
    for k in range(count // 8):
        high, low = split(p_ref[first * OCC + k * CHUNK:first * OCC + (k + 1) * CHUNK, :])
        flipped = jnp.dot(high, wanted, preferred_element_type=jnp.float32)
        flipped = flipped + jnp.dot(low, wanted, preferred_element_type=jnp.float32)
        for m in range(8):
            rows = slice((8 * k + m) * PITCH, (8 * k + m) * PITCH + OCC)
            for g in range(groups):
                turned[g, rows, :] = flipped[m * OCC:(m + 1) * OCC, g * LANES:(g + 1) * LANES]


def low_kernel(distance, p_ref, hot_ref, sent_ref, kept_ref, turned):
    chip = lax.rem(lax.axis_index("x") + distance, 4)
    y = lax.axis_index("y")
    core = lax.axis_index("core")
    wanted = hot_ref[:, pl.ds(pl.multiple_of(chip * 2 * LANES, LANES), 2 * LANES)]
    turn(p_ref, wanted, turned, 0, LOW)
    for side, out_ref in ((1 - core, sent_ref), (core, kept_ref)):
        for e in range(4):
            for z in range(8):
                i = 8 * lax.rem(y + e, 4) + z
                straight = p_ref[pl.ds(pl.multiple_of(i * OCC, OCC), LOW), columns(2 * chip + side)]
                slot = slice((8 * e + z) * LOW, (8 * e + z + 1) * LOW)
                out_ref[slot, :] = straight + turned[side, pl.ds(i, LOW, stride=PITCH), :]


def high_kernel(p_ref, hot_ref, sent_ref, kept_ref, turned):
    x = lax.axis_index("x")
    y = lax.axis_index("y")
    core = lax.axis_index("core")
    turn(p_ref, hot_ref[...], turned, LOW, HIGH)
    for e in range(4):
        for z in range(8):
            i = 8 * lax.rem(y + e, 4) + z
            rows = pl.ds(pl.multiple_of(i * OCC + LOW, HIGH), HIGH)
            for side, out_ref in ((1 - core, sent_ref), (core, kept_ref)):
                for d in range(4):
                    g = 2 * lax.rem(x + d, 4) + side
                    value = p_ref[rows, columns(g)] + turned[g, pl.ds(i, HIGH, stride=PITCH), :]
                    out_ref[e, d, z * HIGH:(z + 1) * HIGH, :] = value


def mirrored(kernel, shape, scratch, partial, hot):
    out = jax.ShapeDtypeStruct(shape, jnp.float32)
    return pl.pallas_call(
        kernel,
        out_shape=(out, out),
        scratch_shapes=[pltpu.VMEM(scratch, jnp.float32)],
        compiler_params=pltpu.CompilerParams(vmem_limit_bytes=16 * 2**20),
        cost_estimate=pl.CostEstimate(flops=PAIRS**3, bytes_accessed=5 * 2**20, transcendentals=0),
    )(partial, hot)


def low_piece(partial, hot, distance):
    def kernel(*refs):
        low_kernel(distance, *refs)

    return mirrored(kernel, (OCC * LOW, LANES), (2, LOW * PITCH, LANES), partial, hot)


def join_kernel(*refs):
    joined_ref = refs[-1]
    for part, rows in enumerate((slice(0, LOW), slice(LOW, OCC))):
        own, a, b, c = refs[4 * part:4 * part + 4]
        total = (own[...] + a[...]) + (b[...] + c[...])
        joined_ref[:, rows, :] = total.reshape(8, rows.stop - rows.start, LANES)


def gram_entry(errors, k, l, lane, message):
    value = jnp.sum(errors[k] * errors[l], keepdims=True)
    return jnp.where(lane == HIST * k + l, value, message)


def prepare_kernel(hist_ref, den_ref, errors_ref, following_ref, den_out_ref, message_ref):
    lane = lax.broadcasted_iota(jnp.int32, (8, LANES), 1)
    errors = [hist_ref[k + 1] - hist_ref[k] for k in range(HIST - 1)]
    message = jnp.zeros((8, LANES), jnp.float32)
    for k in range(HIST - 1):
        errors_ref[k] = errors[k]
        following_ref[k] = hist_ref[k + 1]
        for l in range(k + 1):
            message = gram_entry(errors, k, l, lane, message)
    den_out_ref[...] = den_ref[...]
    message_ref[...] = message


def gram_kernel(parts_ref, den_ref, errors_ref, following_ref, early_ref, update_ref, message_ref):
    total = parts_ref[0]
    for s in range(1, 8):
        total = total + parts_ref[s]
    update = total / den_ref[...]
    update_ref[...] = update
    errors = [errors_ref[k] for k in range(HIST - 1)] + [update - following_ref[HIST - 2]]
    lane = lax.broadcasted_iota(jnp.int32, (8, LANES), 1)
    message = early_ref[...]
    for l in range(HIST):
        message = gram_entry(errors, HIST - 1, l, lane, message)
    for s in range(32):
        message_ref[s * 8:(s + 1) * 8, :] = message


def tail_kernel(grams_ref, update_ref, following_ref, out_ref, coef_ref):
    row = jnp.sum(grams_ref[...], axis=0, keepdims=True)
    spread = (1, LANES)
    a = [[jnp.broadcast_to(row[:, HIST * k + l:HIST * k + l + 1], spread) for l in range(k + 1)] for k in range(HIST)]
    trace = a[0][0]
    for k in range(1, HIST):
        trace = trace + a[k][k]
    ridge = 1e-06 * trace / HIST
    for k in range(HIST):
        a[k][k] = a[k][k] + ridge
    low = [[None] * HIST for _ in range(HIST)]
    inverse = [None] * HIST
    for k in range(HIST):
        pivot = a[k][k]
        for m in range(k):
            pivot = pivot - low[k][m] * low[k][m]
        inverse[k] = 1.0 / jnp.sqrt(pivot)
        for n in range(k + 1, HIST):
            entry = a[n][k]
            for m in range(k):
                entry = entry - low[n][m] * low[k][m]
            low[n][k] = entry * inverse[k]
    half = [None] * HIST
    for k in range(HIST):
        value = jnp.ones(spread, jnp.float32)
        for m in range(k):
            value = value - low[k][m] * half[m]
        half[k] = value * inverse[k]
    whole = [None] * HIST
    for k in reversed(range(HIST)):
        value = half[k]
        for m in range(k + 1, HIST):
            value = value - low[m][k] * whole[m]
        whole[k] = value * inverse[k]
    total = whole[0]
    for k in range(1, HIST):
        total = total + whole[k]
    lane = lax.broadcasted_iota(jnp.int32, spread, 1)
    weights = [whole[k] / total for k in range(HIST)]
    coefficients = jnp.zeros(spread, jnp.float32)
    for k in range(HIST):
        coefficients = jnp.where(lane == k, weights[k], coefficients)
    coef_ref[...] = coefficients[:, :HIST]
    out = weights[HIST - 1] * update_ref[...]
    for k in range(HIST - 1):
        out = out + weights[k] * following_ref[k]
    out_ref[...] = out


def shift(value, axis, distance):
    return lax.ppermute(value, axis, [(i, (i + distance) % 4) for i in range(4)])


def product(a, b):
    return lax.dot_general(
        a,
        b,
        (((0,), (0,)), ((), ())),
        precision=lax.Precision.HIGH,
        preferred_element_type=jnp.float32,
    )


def step(amplitudes, integrals, denominators, history):
    block = jax.ShapeDtypeStruct((OCC, LANES), jnp.float32)
    slabs = jax.ShapeDtypeStruct((HIST - 1, OCC, LANES), jnp.float32)
    errors, following, divisors, early = pl.pallas_call(
        prepare_kernel,
        out_shape=(slabs, slabs, block, jax.ShapeDtypeStruct((8, LANES), jnp.float32)),
        cost_estimate=pl.CostEstimate(flops=2**18, bytes_accessed=2**19, transcendentals=0),
        compiler_params=SMALL,
        name="prepare",
    )(history, denominators)
    hot = pl.pallas_call(
        hot_kernel,
        out_shape=jax.ShapeDtypeStruct((PAIRS, PAIRS), jnp.bfloat16),
        compiler_params=SMALL,
        cost_estimate=pl.CostEstimate(flops=2**20, bytes_accessed=2**21, transcendentals=0),
        name="hot",
    )()
    partial = product(amplitudes[:PAIRS // 2], integrals[:PAIRS // 2])
    partial = partial + product(amplitudes[PAIRS // 2:], integrals[PAIRS // 2:])
    pieces = {}
    for distance in (2, 1, 3, 0):
        sent, kept = low_piece(partial, hot, distance)
        came = lax.ppermute(sent, "core", [(0, 1), (1, 0)])
        pieces[distance] = (kept, came)
    low = pieces[0][0] + pieces[0][1]
    for d in (2, 1, 3):
        low = low + shift(pieces[d][0] + pieces[d][1], "x", d)
    low = low.reshape(4, 8 * LOW, LANES)
    sent, kept = mirrored(high_kernel, (4, 4, 8 * HIGH, LANES), (8, HIGH * PITCH, LANES), partial, hot)
    came = lax.ppermute(sent, "core", [(0, 1), (1, 0)])
    high = kept[0] + came[0]
    for e in (2, 1, 3):
        high = high + shift(kept[e] + came[e], "y", e)
    quarters = [high[0]]
    for d in (2, 1, 3):
        quarters.append(shift(high[d], "x", d))
    parts = [low[0]]
    for e in (2, 1, 3):
        parts.append(shift(low[e], "y", e))
    parts += quarters
    rows = pl.pallas_call(
        join_kernel,
        out_shape=jax.ShapeDtypeStruct((8, OCC, LANES), jnp.float32),
        compiler_params=SMALL,
        name="join",
    )(*parts)
    parts = lax.all_to_all(rows, "z", 0, 0, tiled=True)
    update, message = pl.pallas_call(
        gram_kernel,
        out_shape=(block, jax.ShapeDtypeStruct((256, LANES), jnp.float32)),
        compiler_params=SMALL,
        name="gram",
    )(parts, divisors, errors, following, early)
    grams = lax.all_to_all(message, ("x", "core", "y", "z"), 0, 0, tiled=True)
    extrapolated, coefficients = pl.pallas_call(
        tail_kernel,
        out_shape=(block, jax.ShapeDtypeStruct((1, HIST), jnp.float32)),
        compiler_params=SMALL,
        name="tail",
    )(grams, update, following)
    return extrapolated, coefficients.reshape(HIST)


def solution(mesh):
    cores = Mesh(mesh.devices.reshape(4, 2, 4, 8), ("x", "core", "y", "z"))
    pairs = P(("x", "core", "y", "z"), None)
    return jax.shard_map(
        step,
        mesh=cores,
        in_specs=(pairs, pairs, P(("y", "z"), ("x", "core")), P(None, ("y", "z"), ("x", "core"))),
        out_specs=(P(("y", "z"), ("x", "core")), P()),
        check_vma=False,
    )
```
